512 devices in a mesh: freq: 16 (over x, y_hi, core), tm: 32 (over y_lo, z).
Axes of the slice: x: 4, y: 8 (y_hi: 2, y_lo: 4; y = y_hi * 4 + y_lo), z: 8, core: 2. Of those that a mesh axis runs over, the one named last changes fastest.
Arguments:
- visibilities: float32 [32, 8, 4096], P('freq', None, 'tm'), may hold values from -6 to 6
- coherencies: bfloat16 [32, 8, 8, 4096], P('freq', None, None, 'tm'), may hold values from -2.09375 to 2.09375
- pairs: int32 [2, 4096], P(None, 'tm'), may hold values from 0 to 511, as said below
- gains_start: float32 [32, 8, 8, 512], P('freq'), may hold values from -0.9 to 1.9
- duals_start: float32 [32, 8, 8, 512], P('freq'), may hold values from -12 to 12
- poly_start: float32 [4, 8, 8, 512], replicated, may hold values from -0.6 to 1.6
Outputs:
- gains: float32 [32, 8, 8, 512], P('freq')
- duals: float32 [32, 8, 8, 512], P('freq')
- polynomial: float32 [4, 8, 8, 512], replicated
The draws below stay inside these ranges and needn't reach their ends.
Inputs may be any that keep to these rules, and one draw needn't show every extreme that they name: `pairs`: each row names two different stations.
All inputs are finite; a program needn't handle non-finite values.
Results may differ from the reference program's by a relative error of at most 0.0003.
Values sent between devices are 32-bit elements; how exact they have to be, the bound alone decides.
No kernel may reach another device: no remote copies, remote signals or barrier semaphores. Data moves between devices by JAX's collectives and lax.ppermute only.
A program may use at most 64 MiB of HBM per device.

```python
from functools import partial
import jax
import jax.numpy as jnp
from jax import lax

STATIONS = 512
DIRS = 8
POLY = 4
ITERS = 2
STEPS = 1
NCHAN = 32
ROWS_ALL = 4096


def identity_mask():
    index = jnp.arange(8)
    return ((index == 0) | (index == 3)).astype(jnp.float32)[None, :, None, None]


def draw_pairs(key, part):
    first_key, second_key = jax.random.split(jax.random.fold_in(key, 11))
    first = jax.random.randint(first_key, (ROWS_ALL,), 0, STATIONS)
    offset = jax.random.randint(second_key, (ROWS_ALL,), 1, STATIONS)
    second = (first + offset) % STATIONS
    return jnp.stack([first, second]).astype(jnp.int32)


def draw_gains_start(key, part):
    noise_key = jax.random.fold_in(jax.random.fold_in(key, 23), 0)
    shape = (NCHAN, 8, DIRS, STATIONS)
    noise = 0.3 * jnp.clip(jax.random.normal(noise_key, shape, jnp.float32), -3.0, 3.0)
    return noise + identity_mask()


def draw_poly_start(key, part):
    noise_key = jax.random.fold_in(jax.random.fold_in(key, 37), 0)
    shape = (POLY, 8, DIRS, STATIONS)
    noise = 0.2 * jnp.clip(jax.random.normal(noise_key, shape, jnp.float32), -3.0, 3.0)
    leading = (jnp.arange(POLY) == 0).astype(jnp.float32)[:, None, None, None]
    return noise + leading * identity_mask()


def block_levels(own_key, extent, pieces, low, largest):
    def one(dim, shards_of):
        heights = jax.random.uniform(jax.random.fold_in(jax.random.fold_in(own_key, 6), dim), (shards_of,), jnp.float32, low / len(pieces), largest / len(pieces))
        return jnp.repeat(jnp.exp(heights), extent[dim] // shards_of).reshape((-1,) + (1,) * (len(extent) - dim - 1))

    gain = one(*pieces[0])
    for cut in pieces[1:]:
        gain = gain * one(*cut)
    return gain


def normal_values(stream_key, dims, scale, most, cuts=(), kind=jnp.bfloat16):
    entries = jax.random.normal(stream_key, dims, jnp.float32) * scale
    if len(cuts) > 0:
        entries = block_levels(stream_key, dims, cuts, -0.22, 0.18) * entries
    return jnp.clip(entries, min=-most, max=most).astype(kind)


def setup_inputs(seed: int = 0) -> dict:
    splits = jax.random.split(jax.random.key(seed), 7)
    return {
        "visibilities": normal_values(splits[0], (NCHAN, 8, ROWS_ALL), 1.0, 6.0, ((0, 16), (2, 32)), jnp.float32),
        "coherencies": normal_values(splits[1], (NCHAN, 8, DIRS, ROWS_ALL), 0.35, 2.09375, ((0, 16), (3, 32))),
        "pairs": draw_pairs(jax.random.fold_in(splits[6], 71), 0),
        "gains_start": draw_gains_start(jax.random.fold_in(splits[6], 71), 0),
        "duals_start": normal_values(splits[4], (NCHAN, 8, DIRS, STATIONS), 2.0, 12.0, ((0, 16),), jnp.float32),
        "poly_start": draw_poly_start(jax.random.fold_in(splits[6], 71), 0),
    }


RHO = 16.0
HIGHEST = lax.Precision.HIGHEST

def split(block):
    return ([block[i] for i in range(4)], [block[i + 4] for i in range(4)])

def join(matrix):
    return jnp.stack(matrix[0] + matrix[1])

def adjoint(matrix):
    real_part, imag_part = matrix
    return ([real_part[0], real_part[2], real_part[1], real_part[3]], [-imag_part[0], -imag_part[2], -imag_part[1], -imag_part[3]])

def product(left, right):
    left_real, left_imag = left
    right_real, right_imag = right
    out_real = []
    out_imag = []
    for row in range(2):
        for column in range(2):
            first = 2 * row
            out_real.append(left_real[first] * right_real[column] - left_imag[first] * right_imag[column] + left_real[first + 1] * right_real[column + 2] - left_imag[first + 1] * right_imag[column + 2])
            out_imag.append(left_real[first] * right_imag[column] + left_imag[first] * right_real[column] + left_real[first + 1] * right_imag[column + 2] + left_imag[first + 1] * right_real[column + 2])
    return (out_real, out_imag)

def normal(matrix):
    real_part, imag_part = matrix
    top_left = real_part[0] ** 2 + imag_part[0] ** 2 + real_part[1] ** 2 + imag_part[1] ** 2
    bottom_right = real_part[2] ** 2 + imag_part[2] ** 2 + real_part[3] ** 2 + imag_part[3] ** 2
    cross_real = real_part[0] * real_part[2] + imag_part[0] * imag_part[2] + real_part[1] * real_part[3] + imag_part[1] * imag_part[3]
    cross_imag = imag_part[0] * real_part[2] - real_part[0] * imag_part[2] + imag_part[1] * real_part[3] - real_part[1] * imag_part[3]
    return jnp.stack([top_left, bottom_right, cross_real, cross_imag])

def data_sums(gains, coherencies, visibilities, pairs):
    jones_first = split(jnp.take(gains, pairs[0], axis=2))
    jones_second = split(jnp.take(gains, pairs[1], axis=2))
    skymodel = split(coherencies.astype(jnp.float32))
    left = product(jones_first, skymodel)
    right = product(skymodel, adjoint(jones_second))
    model = jnp.sum(join(product(left, adjoint(jones_second))), axis=1)
    residual = split((visibilities - model)[:, None, :])
    first_terms = jnp.concatenate([join(product(residual, adjoint(right))), normal(right)], axis=0)
    second_terms = jnp.concatenate([join(product(adjoint(residual), left)), normal(adjoint(left))], axis=0)
    terms = jnp.concatenate([first_terms, second_terms], axis=2)
    stations = jnp.concatenate([pairs[0], pairs[1]]).astype(jnp.int32)
    flat = terms.reshape(-1, terms.shape[2]).T
    summed = jax.ops.segment_sum(flat, stations, num_segments=gains.shape[2])
    return summed.T.reshape(12, gains.shape[1], gains.shape[2])

def update(gains, duals, prior, sums, damping):
    direction = split(sums[:8] - duals - RHO * (gains - prior))
    top_left, bottom_right, cross_real, cross_imag = (sums[8], sums[9], sums[10], sums[11])
    shift = damping * 0.5 * (top_left + bottom_right) + RHO
    upper = top_left + shift
    lower = bottom_right + shift
    determinant = upper * lower - cross_real * cross_real - cross_imag * cross_imag
    zeros = jnp.zeros_like(determinant)
    inverse = ([lower / determinant, -cross_real / determinant, -cross_real / determinant, upper / determinant], [zeros, -cross_imag / determinant, cross_imag / determinant, zeros])
    return gains + join(product(direction, inverse))

def basis_weights(count):
    position = (2.0 * jnp.arange(count).astype(jnp.float32) + 1.0) / count - 1.0
    basis = jnp.stack([jnp.ones_like(position), position, 1.5 * position * position - 0.5, 2.5 * position * position * position - 1.5 * position], axis=1)
    gram = jnp.dot(basis.T, basis, precision=HIGHEST)
    factor = jnp.linalg.cholesky(gram)
    weights = jax.scipy.linalg.cho_solve((factor, True), basis.T)
    return (basis, weights)

def reference(visibilities, coherencies, pairs, gains_start, duals_start, poly_start):
    basis, weights = basis_weights(gains_start.shape[0])
    prior = jnp.einsum('fj,jcks->fcks', basis, poly_start, precision=HIGHEST)
    gains, duals, polynomial = (gains_start, duals_start, poly_start)

    def channel(items):
        return data_sums(items[0], items[1], items[2], pairs)
    for outer in range(STEPS):
        for inner in range(ITERS):
            sums = lax.map(channel, (gains, coherencies, visibilities))
            gains = jax.vmap(partial(update, damping=12.0 * 0.5 ** inner))(gains, duals, prior, sums)
        mixed = gains + duals / RHO
        polynomial = jnp.einsum('jf,fcks->jcks', weights, mixed, precision=HIGHEST)
        prior = jnp.einsum('fj,jcks->fcks', basis, polynomial, precision=HIGHEST)
        duals = duals + RHO * (gains - prior)
    return (gains, duals, polynomial)
```

```python
import functools

import jax
import jax.numpy as jnp
import numpy as np
from jax import lax
from jax.experimental import pallas as pl
from jax.experimental.pallas import tpu as pltpu
from jax.sharding import PartitionSpec as P

ITERS = 2
RHO = 16.0
CHANS = 2
DIRS = 8
STATIONS = 512
ROWS = 128
POLY = 4
LANES = 128
CUTS = STATIONS // LANES
F32 = jnp.float32
BF16 = jnp.bfloat16


def adjoint(matrix):
    re, im = matrix
    return ([re[0], re[2], re[1], re[3]], [-im[0], -im[2], -im[1], -im[3]])


def product(left, right):
    lr, li = left
    rr, ri = right
    out_re, out_im = [], []
    for row in range(2):
        for col in range(2):
            a = 2 * row
            out_re.append(lr[a] * rr[col] - li[a] * ri[col] + lr[a + 1] * rr[col + 2] - li[a + 1] * ri[col + 2])
            out_im.append(lr[a] * ri[col] + li[a] * rr[col] + lr[a + 1] * ri[col + 2] + li[a + 1] * rr[col + 2])
    return (out_re, out_im)


def normal(matrix):
    re, im = matrix
    return [
        re[0] ** 2 + im[0] ** 2 + re[1] ** 2 + im[1] ** 2,
        re[2] ** 2 + im[2] ** 2 + re[3] ** 2 + im[3] ** 2,
        re[0] * re[2] + im[0] * im[2] + re[1] * re[3] + im[1] * im[3],
        im[0] * re[2] - re[0] * im[2] + im[1] * re[3] - re[1] * im[3],
    ]


def two_parts(x):
    high = x.astype(BF16)
    low = (x - high.astype(F32)).astype(BF16)
    return jnp.concatenate([high, low], axis=0)


def one_hot(pairs_ref):
    station = lax.broadcasted_iota(jnp.int32, (STATIONS, ROWS), 0)
    marks = [jnp.where(station == pairs_ref[i : i + 1, :], 1.0, 0.0) for i in range(2)]
    return jnp.concatenate(marks, axis=1).astype(BF16)


def sums_kernel(gathered, gains_ref, coh_ref, vis_ref, pairs_ref, out_ref, at_p, at_q, terms_p, terms_q, summed):
    hot = one_hot(pairs_ref)
    if gathered:
        rows = jnp.concatenate(
            [
                jnp.concatenate([gains_ref[k * CUTS + q] for q in range(CUTS)], axis=1)
                for k in range(DIRS)
            ],
            axis=0,
        )
    else:
        rows = gains_ref[...].reshape(CHANS * 8 * DIRS, STATIONS)
    count = rows.shape[0]
    found = jnp.dot(two_parts(rows), hot, preferred_element_type=F32)
    found = found[:count] + found[count:]
    at_p[...] = found[:, :ROWS]
    at_q[...] = found[:, ROWS:]

    def picked(ref, c, i):
        if gathered:
            return ref[pl.ds(c * 8 + i, DIRS, stride=CHANS * 8), :]
        return ref[pl.ds((c * 8 + i) * DIRS, DIRS), :]

    for c in range(CHANS):
        first = ([picked(at_p, c, i) for i in range(4)], [picked(at_p, c, i + 4) for i in range(4)])
        second = ([picked(at_q, c, i) for i in range(4)], [picked(at_q, c, i + 4) for i in range(4)])
        sky = [coh_ref[c, i].astype(F32) for i in range(8)]
        sky = (sky[:4], sky[4:])
        left = product(first, sky)
        right = product(sky, adjoint(second))
        model = product(left, adjoint(second))
        model = [jnp.sum(part, axis=0, keepdims=True) for part in model[0] + model[1]]
        rest = [
            jnp.broadcast_to(vis_ref[c, pl.ds(i, 1), :] - model[i], (DIRS, ROWS)) for i in range(8)
        ]
        rest = (rest[:4], rest[4:])
        grad_p = product(rest, adjoint(right))
        grad_q = product(adjoint(rest), left)
        for ref, terms in (
            (terms_p, grad_p[0] + grad_p[1] + normal(right)),
            (terms_q, grad_q[0] + grad_q[1] + normal(adjoint(left))),
        ):
            for i, term in enumerate(terms):
                ref[pl.ds((c * 12 + i) * DIRS, DIRS), :] = term
    terms = jnp.concatenate([terms_p[...], terms_q[...]], axis=1)
    count = terms.shape[0]
    total = lax.dot_general(
        two_parts(terms), hot, (((1,), (1,)), ((), ())), preferred_element_type=F32
    )
    total = total[:count] + total[count:]
    for q in range(CUTS):
        summed[q] = total[:, q * LANES : (q + 1) * LANES]
    for k in range(DIRS):
        for q in range(CUTS):
            out_ref[k * CUTS + q] = summed[q, pl.ds(k, CHANS * 12, stride=DIRS), :]


def share_sums(gains, coherencies, visibilities, pairs, gathered):
    rows = CHANS * 8 * DIRS
    terms = CHANS * 12 * DIRS
    return pl.pallas_call(
        functools.partial(sums_kernel, gathered),
        out_shape=jax.ShapeDtypeStruct((DIRS * CUTS, CHANS * 12, LANES), F32),
        scratch_shapes=[
            pltpu.VMEM((rows, ROWS), F32),
            pltpu.VMEM((rows, ROWS), F32),
            pltpu.VMEM((terms, ROWS), F32),
            pltpu.VMEM((terms, ROWS), F32),
            pltpu.VMEM((CUTS, terms, LANES), F32),
        ],
        name="sums",
    )(gains, coherencies, visibilities, pairs)


def basis_of(channel, count):
    x = (2.0 * channel.astype(F32) + 1.0) / count - 1.0
    return [1.0 + 0.0 * x, x, 1.5 * x * x - 0.5, 2.5 * x * x * x - 1.5 * x]


def inverse_gram(count):
    x = (2.0 * np.arange(count) + 1.0) / count - 1.0
    basis = np.stack([np.ones_like(x), x, 1.5 * x * x - 0.5, 2.5 * x**3 - 1.5 * x], axis=1)
    return np.linalg.inv(basis.T @ basis)


def weights_of(basis, gram):
    return [sum(float(gram[j, i]) * basis[i] for i in range(POLY)) for j in range(POLY)]


def own_kernel(count, index_ref, gains_ref, duals_ref, poly_ref, out_ref):
    freq, place = index_ref[0], index_ref[1]
    k = place // CUTS
    lanes = pl.ds(pl.multiple_of((place % CUTS) * LANES, LANES), LANES)
    chosen = lax.broadcasted_iota(jnp.int32, (DIRS, LANES), 0) == k

    def row(tile):
        return jnp.sum(jnp.where(chosen, tile, 0.0), axis=0, keepdims=True)

    for c in range(CHANS):
        basis = basis_of(freq * CHANS + c, count)
        for i in range(8):
            at = pl.ds(c * 8 + i, 1)
            out_ref[0, at, :] = row(gains_ref[c, i, :, lanes])
            out_ref[1, at, :] = row(duals_ref[c, i, :, lanes])
            prior = basis[0] * poly_ref[0, i, :, lanes]
            for j in range(1, POLY):
                prior += basis[j] * poly_ref[j, i, :, lanes]
            out_ref[2, at, :] = row(prior)


SMEM = pl.BlockSpec(memory_space=pltpu.SMEM)
VMEM = pl.BlockSpec(memory_space=pltpu.VMEM)


def own_share(index, gains, duals, poly, count):
    return pl.pallas_call(
        functools.partial(own_kernel, count),
        out_shape=jax.ShapeDtypeStruct((3, CHANS * 8, LANES), F32),
        in_specs=[SMEM, VMEM, VMEM, VMEM],
        name="own",
    )(index, gains, duals, poly)


def both(ref, i, step):
    return ref[pl.ds(i, CHANS, stride=step), :]


def updated(sums_ref, own_ref, gains_ref, damping, arrived, put):
    total = arrived[0]
    for n in range(1, arrived.shape[0]):
        total = total + arrived[n]
    sums_ref[...] = total
    gains = [both(gains_ref, i, 8) for i in range(8)]
    way = [
        both(sums_ref, i, 12) - both(own_ref.at[1], i, 8) - RHO * (gains[i] - both(own_ref.at[2], i, 8))
        for i in range(8)
    ]
    top, bottom, cross_re, cross_im = [both(sums_ref, i, 12) for i in range(8, 12)]
    shift = damping * 0.5 * (top + bottom) + RHO
    upper = top + shift
    lower = bottom + shift
    scale = 1.0 / (upper * lower - cross_re * cross_re - cross_im * cross_im)
    zeros = jnp.zeros_like(scale)
    inverse = (
        [lower * scale, -cross_re * scale, -cross_re * scale, upper * scale],
        [zeros, -cross_im * scale, cross_im * scale, zeros],
    )
    step = product((way[:4], way[4:]), inverse)
    step = step[0] + step[1]
    for i in range(8):
        put[pl.ds(i, CHANS, stride=8), :] = gains[i] + step[i]


def first_kernel(damping, arrived, own_ref, out_ref, sums_ref, new):
    updated(sums_ref, own_ref, own_ref.at[0], damping, arrived, new)
    value = new[...]
    for n in range(out_ref.shape[0]):
        out_ref[n] = value


def last_kernel(damping, count, gram, index_ref, arrived, own_ref, gains_ref, fit_ref, new, sums_ref):
    updated(sums_ref, own_ref, gains_ref, damping, arrived, new)
    mixed = new[...] + own_ref[1] / RHO
    weights = [weights_of(basis_of(index_ref[0] * CHANS + c, count), gram) for c in range(CHANS)]
    for core in range(2):
        parts = [
            sum(weights[c][2 * core + j] * mixed[c * 8 : (c + 1) * 8] for c in range(CHANS))
            for j in range(2)
        ]
        part = jnp.concatenate(parts, axis=0)
        for n in range(core, fit_ref.shape[0], 2):
            fit_ref[n] = part


def joined_kernel(arrived, gains_ref, out_ref):
    total = arrived[0]
    for n in range(1, arrived.shape[0]):
        total = total + arrived[n]
    gains = gains_ref[...]
    for n in range(out_ref.shape[0]):
        out_ref[n, pl.ds(0, 16), :] = gains
        out_ref[n, pl.ds(16, 16), :] = total


def end_kernel(count, index_ref, all_ref, other_ref, duals_ref, gains_out, duals_out, poly_out):
    freq = index_ref[0]
    core = freq % 2
    basis = [basis_of(freq * CHANS + c, count) for c in range(CHANS)]
    mine = [[jnp.where(core == 0, basis[c][j], basis[c][j + 2]) for j in range(2)] for c in range(CHANS)]
    his = [[jnp.where(core == 0, basis[c][j + 2], basis[c][j]) for j in range(2)] for c in range(CHANS)]
    every = CUTS * 32
    half = CUTS * 16
    for i in range(8):
        for q in range(CUTS):
            lanes = pl.ds(q * LANES, LANES)
            own = [all_ref[pl.ds(q * 32 + 16 + j * 8 + i, DIRS, stride=every), :] for j in range(2)]
            far = [other_ref[pl.ds(q * 16 + j * 8 + i, DIRS, stride=half), :] for j in range(2)]
            for j in range(2):
                poly_out[2 * core + j, i, :, lanes] = own[j]
                poly_out[2 - 2 * core + j, i, :, lanes] = far[j]
            for c in range(CHANS):
                gains = all_ref[pl.ds(q * 32 + c * 8 + i, DIRS, stride=every), :]
                gains_out[c, i, :, lanes] = gains
                prior = mine[c][0] * own[0] + mine[c][1] * own[1] + his[c][0] * far[0] + his[c][1] * far[1]
                duals_out[c, i, :, lanes] = duals_ref[c, i, :, lanes] + RHO * (gains - prior)


def exchanged(x, axis):
    return lax.all_to_all(x, axis, split_axis=0, concat_axis=0, tiled=True)


def shards(visibilities, coherencies, pairs, gains_start, duals_start, poly_start):
    freqs, times = lax.axis_size("freq"), lax.axis_size("tm")
    count = CHANS * freqs
    index = jnp.stack([lax.axis_index("freq"), lax.axis_index("tm")]).astype(jnp.int32)
    share = jax.ShapeDtypeStruct((CHANS * 8, LANES), F32)
    sums_scratch = pltpu.VMEM((CHANS * 12, LANES), F32)
    new_scratch = pltpu.VMEM((CHANS * 8, LANES), F32)

    own = own_share(index, gains_start, duals_start, poly_start, count)
    sums = exchanged(share_sums(gains_start, coherencies, visibilities, pairs, False), "tm")
    copies = pl.pallas_call(
        functools.partial(first_kernel, 12.0),
        out_shape=jax.ShapeDtypeStruct((times, CHANS * 8, LANES), F32),
        scratch_shapes=[sums_scratch, new_scratch],
        name="first",
    )(sums, own)
    gains = exchanged(copies, "tm")
    sums = exchanged(share_sums(gains, coherencies, visibilities, pairs, True), "tm")
    fits, mine = pl.pallas_call(
        functools.partial(last_kernel, 6.0, count, inverse_gram(count)),
        out_shape=(jax.ShapeDtypeStruct((freqs, 16, LANES), F32), share),
        in_specs=[SMEM, VMEM, VMEM, VMEM],
        scratch_shapes=[sums_scratch],
        name="last",
    )(index, sums, own, copies[0])
    fits = exchanged(fits, "freq")
    copies = pl.pallas_call(
        joined_kernel,
        out_shape=jax.ShapeDtypeStruct((times, 32, LANES), F32),
        name="joined",
    )(fits, mine)
    everything = exchanged(copies, "tm")
    other = lax.ppermute(everything[:, 16:], "freq", [(i, i ^ 1) for i in range(freqs)])
    block = (CHANS, 8, DIRS, STATIONS)
    return pl.pallas_call(
        functools.partial(end_kernel, count),
        out_shape=(
            jax.ShapeDtypeStruct(block, F32),
            jax.ShapeDtypeStruct(block, F32),
            jax.ShapeDtypeStruct((POLY, 8, DIRS, STATIONS), F32),
        ),
        in_specs=[SMEM, VMEM, VMEM, VMEM],
        name="end",
    )(index, everything.reshape(times * 32, LANES), other.reshape(times * 16, LANES), duals_start)


def solution(mesh):
    placed = (
        P("freq", None, "tm"),
        P("freq", None, None, "tm"),
        P(None, "tm"),
        P("freq", None, None, None),
        P("freq", None, None, None),
        P(),
    )
    return jax.shard_map(
        shards,
        mesh=mesh,
        in_specs=placed,
        out_specs=(P("freq", None, None, None), P("freq", None, None, None), P()),
        check_vma=False,
    )
```

```python
import functools

import jax
import jax.numpy as jnp
import numpy as np
from jax import lax
from jax.experimental import pallas as pl
from jax.experimental.pallas import tpu as pltpu
from jax.sharding import PartitionSpec as P

ITERS = 2
RHO = 16.0
CHANS = 2
DIRS = 8
STATIONS = 512
ROWS = 128
POLY = 4
LANES = 128
CUTS = STATIONS // LANES
F32 = jnp.float32
BF16 = jnp.bfloat16


def adjoint(matrix):
    re, im = matrix
    return ([re[0], re[2], re[1], re[3]], [-im[0], -im[2], -im[1], -im[3]])


def product(left, right):
    lr, li = left
    rr, ri = right
    out_re, out_im = [], []
    for row in range(2):
        for col in range(2):
            a = 2 * row
            out_re.append(lr[a] * rr[col] - li[a] * ri[col] + lr[a + 1] * rr[col + 2] - li[a + 1] * ri[col + 2])
            out_im.append(lr[a] * ri[col] + li[a] * rr[col] + lr[a + 1] * ri[col + 2] + li[a + 1] * rr[col + 2])
    return (out_re, out_im)


def normal(matrix):
    re, im = matrix
    return [
        re[0] ** 2 + im[0] ** 2 + re[1] ** 2 + im[1] ** 2,
        re[2] ** 2 + im[2] ** 2 + re[3] ** 2 + im[3] ** 2,
        re[0] * re[2] + im[0] * im[2] + re[1] * re[3] + im[1] * im[3],
        im[0] * re[2] - re[0] * im[2] + im[1] * re[3] - re[1] * im[3],
    ]


def two_parts(x):
    high = x.astype(BF16)
    low = (x - high.astype(F32)).astype(BF16)
    return jnp.concatenate([high, low], axis=0)


def one_hot(pairs_ref):
    station = lax.broadcasted_iota(jnp.int32, (STATIONS, ROWS), 0)
    marks = [jnp.where(station == pairs_ref[i : i + 1, :], 1.0, 0.0) for i in range(2)]
    return jnp.concatenate(marks, axis=1).astype(BF16)


SMEM = pl.BlockSpec(memory_space=pltpu.SMEM)
VMEM = pl.BlockSpec(memory_space=pltpu.VMEM)

def call(kernel, outs, *args, scratch=(), fast=None, slow_outs=False, limit=12 << 20, name=None):
    fast = range(len(args)) if fast is None else fast
    args = [
        pltpu.with_memory_space_constraint(a, pltpu.MemorySpace.VMEM) if n in fast else a
        for n, a in enumerate(args)
    ]
    kind = (lambda shape: jax.ShapeDtypeStruct(shape, F32)) if slow_outs else (lambda shape: pltpu.VMEM(shape, F32))
    many = isinstance(outs, list)
    return pl.pallas_call(
        kernel,
        out_shape=tuple(kind(o) for o in outs) if many else kind(outs),
        in_specs=[SMEM if a.dtype == jnp.int32 and a.ndim == 1 else VMEM for a in args],
        out_specs=tuple(VMEM for _ in outs) if many else VMEM,
        scratch_shapes=list(scratch),
        compiler_params=pltpu.CompilerParams(vmem_limit_bytes=limit),
        name=name,
    )(*args)


def sums_kernel(gathered, gains_ref, coh_ref, vis_ref, pairs_ref, out_ref, at_p, at_q, terms_p, terms_q, summed):
    hot = one_hot(pairs_ref)
    if gathered:
        rows = jnp.concatenate(
            [
                jnp.concatenate([gains_ref[k * CUTS + q] for q in range(CUTS)], axis=1)
                for k in range(DIRS)
            ],
            axis=0,
        )
    else:
        rows = gains_ref[...].reshape(CHANS * 8 * DIRS, STATIONS)
    count = rows.shape[0]
    found = jnp.dot(two_parts(rows), hot, preferred_element_type=F32)
    found = found[:count] + found[count:]
    at_p[...] = found[:, :ROWS]
    at_q[...] = found[:, ROWS:]

    def picked(ref, c, i):
        if gathered:
            return ref[pl.ds(c * 8 + i, DIRS, stride=CHANS * 8), :]
        return ref[pl.ds((c * 8 + i) * DIRS, DIRS), :]

    for c in range(CHANS):
        first = ([picked(at_p, c, i) for i in range(4)], [picked(at_p, c, i + 4) for i in range(4)])
        second = ([picked(at_q, c, i) for i in range(4)], [picked(at_q, c, i + 4) for i in range(4)])
        sky = [coh_ref[c, i].astype(F32) for i in range(8)]
        sky = (sky[:4], sky[4:])
        left = product(first, sky)
        right = product(sky, adjoint(second))
        model = product(left, adjoint(second))
        model = [jnp.sum(part, axis=0, keepdims=True) for part in model[0] + model[1]]
        rest = [
            jnp.broadcast_to(vis_ref[c, pl.ds(i, 1), :] - model[i], (DIRS, ROWS)) for i in range(8)
        ]
        rest = (rest[:4], rest[4:])
        grad_p = product(rest, adjoint(right))
        grad_q = product(adjoint(rest), left)
        for ref, terms in (
            (terms_p, grad_p[0] + grad_p[1] + normal(right)),
            (terms_q, grad_q[0] + grad_q[1] + normal(adjoint(left))),
        ):
            for i, term in enumerate(terms):
                ref[pl.ds((c * 12 + i) * DIRS, DIRS), :] = term
    terms = jnp.concatenate([terms_p[...], terms_q[...]], axis=1)
    count = terms.shape[0]
    total = lax.dot_general(
        two_parts(terms), hot, (((1,), (1,)), ((), ())), preferred_element_type=F32
    )
    total = total[:count] + total[count:]
    for q in range(CUTS):
        summed[q] = total[:, q * LANES : (q + 1) * LANES]
    for k in range(DIRS):
        for q in range(CUTS):
            out_ref[k * CUTS + q] = summed[q, pl.ds(k, CHANS * 12, stride=DIRS), :]


def share_sums(gains, coherencies, visibilities, pairs, gathered):
    rows = CHANS * 8 * DIRS
    terms = CHANS * 12 * DIRS
    return call(
        functools.partial(sums_kernel, gathered),
        (DIRS * CUTS, CHANS * 12, LANES),
        gains,
        coherencies,
        visibilities,
        pairs,
        fast=[0] if gathered else [],
        limit=12 << 20 if gathered else 60 << 20,
        scratch=[
            pltpu.VMEM((rows, ROWS), F32),
            pltpu.VMEM((rows, ROWS), F32),
            pltpu.VMEM((terms, ROWS), F32),
            pltpu.VMEM((terms, ROWS), F32),
            pltpu.VMEM((CUTS, terms, LANES), F32),
        ],
        name="sums",
    )


def basis_of(channel, count):
    x = (2.0 * channel.astype(F32) + 1.0) / count - 1.0
    return [1.0 + 0.0 * x, x, 1.5 * x * x - 0.5, 2.5 * x * x * x - 1.5 * x]


def inverse_gram(count):
    x = (2.0 * np.arange(count) + 1.0) / count - 1.0
    basis = np.stack([np.ones_like(x), x, 1.5 * x * x - 0.5, 2.5 * x**3 - 1.5 * x], axis=1)
    return np.linalg.inv(basis.T @ basis)


def weights_of(basis, gram):
    return [sum(float(gram[j, i]) * basis[i] for i in range(POLY)) for j in range(POLY)]


def own_kernel(count, index_ref, gains_ref, duals_ref, poly_ref, out_ref):
    freq, place = index_ref[0], index_ref[1]
    k = place // CUTS
    lanes = pl.ds(pl.multiple_of((place % CUTS) * LANES, LANES), LANES)
    chosen = lax.broadcasted_iota(jnp.int32, (DIRS, LANES), 0) == k

    def row(tile):
        return jnp.sum(jnp.where(chosen, tile, 0.0), axis=0, keepdims=True)

    for c in range(CHANS):
        basis = basis_of(freq * CHANS + c, count)
        for i in range(8):
            at = pl.ds(c * 8 + i, 1)
            out_ref[0, at, :] = row(gains_ref[c, i, :, lanes])
            out_ref[1, at, :] = row(duals_ref[c, i, :, lanes])
            prior = basis[0] * poly_ref[0, i, :, lanes]
            for j in range(1, POLY):
                prior += basis[j] * poly_ref[j, i, :, lanes]
            out_ref[2, at, :] = row(prior)


def both(ref, i, step):
    return ref[pl.ds(i, CHANS, stride=step), :]


def updated(sums_ref, own_ref, gains_ref, damping, arrived, put):
    total = arrived[0]
    for n in range(1, arrived.shape[0]):
        total = total + arrived[n]
    sums_ref[...] = total
    gains = [both(gains_ref, i, 8) for i in range(8)]
    way = [
        both(sums_ref, i, 12) - both(own_ref.at[1], i, 8) - RHO * (gains[i] - both(own_ref.at[2], i, 8))
        for i in range(8)
    ]
    top, bottom, cross_re, cross_im = [both(sums_ref, i, 12) for i in range(8, 12)]
    shift = damping * 0.5 * (top + bottom) + RHO
    upper = top + shift
    lower = bottom + shift
    scale = 1.0 / (upper * lower - cross_re * cross_re - cross_im * cross_im)
    zeros = jnp.zeros_like(scale)
    inverse = (
        [lower * scale, -cross_re * scale, -cross_re * scale, upper * scale],
        [zeros, -cross_im * scale, cross_im * scale, zeros],
    )
    step = product((way[:4], way[4:]), inverse)
    step = step[0] + step[1]
    for i in range(8):
        put[pl.ds(i, CHANS, stride=8), :] = gains[i] + step[i]


def first_kernel(damping, arrived, own_ref, out_ref, new, sums_ref):
    updated(sums_ref, own_ref, own_ref.at[0], damping, arrived, new)
    value = new[...]
    for n in range(out_ref.shape[0]):
        out_ref[n] = value


def last_kernel(damping, count, gram, index_ref, arrived, own_ref, gains_ref, fit_ref, new, sums_ref):
    updated(sums_ref, own_ref, gains_ref, damping, arrived, new)
    mixed = new[...] + own_ref[1] / RHO
    weights = [weights_of(basis_of(index_ref[0] * CHANS + c, count), gram) for c in range(CHANS)]
    for core in range(2):
        parts = [
            sum(weights[c][2 * core + j] * mixed[c * 8 : (c + 1) * 8] for c in range(CHANS))
            for j in range(2)
        ]
        part = jnp.concatenate(parts, axis=0)
        for n in range(core, fit_ref.shape[0], 2):
            fit_ref[n] = part


def joined_kernel(arrived, gains_ref, out_ref):
    total = arrived[0]
    for n in range(1, arrived.shape[0]):
        total = total + arrived[n]
    gains = gains_ref[...]
    for n in range(out_ref.shape[0]):
        out_ref[n, pl.ds(0, 16), :] = gains
        out_ref[n, pl.ds(16, 16), :] = total


def end_kernel(count, index_ref, all_ref, other_ref, duals_ref, gains_out, duals_out, poly_out):
    freq = index_ref[0]
    core = freq % 2
    basis = [basis_of(freq * CHANS + c, count) for c in range(CHANS)]
    mine = [[jnp.where(core == 0, basis[c][j], basis[c][j + 2]) for j in range(2)] for c in range(CHANS)]
    his = [[jnp.where(core == 0, basis[c][j + 2], basis[c][j]) for j in range(2)] for c in range(CHANS)]
    every = CUTS * 32
    half = CUTS * 16
    for i in range(8):
        for q in range(CUTS):
            lanes = pl.ds(q * LANES, LANES)
            own = [all_ref[pl.ds(q * 32 + 16 + j * 8 + i, DIRS, stride=every), :] for j in range(2)]
            far = [other_ref[pl.ds(q * 16 + j * 8 + i, DIRS, stride=half), :] for j in range(2)]
            for j in range(2):
                poly_out[2 * core + j, i, :, lanes] = own[j]
                poly_out[2 - 2 * core + j, i, :, lanes] = far[j]
            for c in range(CHANS):
                gains = all_ref[pl.ds(q * 32 + c * 8 + i, DIRS, stride=every), :]
                gains_out[c, i, :, lanes] = gains
                prior = mine[c][0] * own[0] + mine[c][1] * own[1] + his[c][0] * far[0] + his[c][1] * far[1]
                duals_out[c, i, :, lanes] = duals_ref[c, i, :, lanes] + RHO * (gains - prior)


def exchanged(x, axis):
    return lax.all_to_all(x, axis, split_axis=0, concat_axis=0, tiled=True)


def shards(visibilities, coherencies, pairs, gains_start, duals_start, poly_start):
    freqs, times = lax.axis_size("freq"), lax.axis_size("tm")
    count = CHANS * freqs
    index = jnp.stack([lax.axis_index("freq"), lax.axis_index("tm")]).astype(jnp.int32)
    share = (CHANS * 8, LANES)
    scratch = [pltpu.VMEM((CHANS * 12, LANES), F32)]

    own = call(
        functools.partial(own_kernel, count),
        (3, *share),
        index,
        gains_start,
        duals_start,
        poly_start,
        fast=[],
        name="own",
    )
    sums = exchanged(share_sums(gains_start, coherencies, visibilities, pairs, False), "tm")
    copies, mine = call(
        functools.partial(first_kernel, 12.0), [(times, *share), share], sums, own, scratch=scratch, name="first"
    )
    gains = exchanged(copies, "tm")
    sums = exchanged(share_sums(gains, coherencies, visibilities, pairs, True), "tm")
    fits, mine = call(
        functools.partial(last_kernel, 6.0, count, inverse_gram(count)),
        [(freqs, 16, LANES), share],
        index,
        sums,
        own,
        mine,
        fast=[1, 2, 3],
        scratch=scratch,
        name="last",
    )
    fits = exchanged(fits, "freq")
    copies = call(joined_kernel, (times, 32, LANES), fits, mine, name="joined")
    everything = exchanged(copies, "tm")
    other = lax.ppermute(everything[:, 16:], "freq", [(i, i ^ 1) for i in range(freqs)])
    block = (CHANS, 8, DIRS, STATIONS)
    return call(
        functools.partial(end_kernel, count),
        [block, block, (POLY, 8, DIRS, STATIONS)],
        index,
        everything.reshape(times * 32, LANES),
        other.reshape(times * 16, LANES),
        duals_start,
        fast=[1, 2, 3],
        slow_outs=True,
        name="end",
    )


def solution(mesh):
    placed = (
        P("freq", None, "tm"),
        P("freq", None, None, "tm"),
        P(None, "tm"),
        P("freq", None, None, None),
        P("freq", None, None, None),
        P(),
    )
    return jax.shard_map(
        shards,
        mesh=mesh,
        in_specs=placed,
        out_specs=(P("freq", None, None, None), P("freq", None, None, None), P()),
        check_vma=False,
    )
```

```python
import functools

import jax
import jax.numpy as jnp
import numpy as np
from jax import lax
from jax.experimental import pallas as pl
from jax.experimental.pallas import tpu as pltpu
from jax.sharding import Mesh
from jax.sharding import PartitionSpec as P

ITERS = 2
RHO = 16.0
CHANS = 2
DIRS = 8
STATIONS = 512
ROWS = 128
POLY = 4
LANES = 128
CUTS = STATIONS // LANES
GROUPS = 4
PAIR = DIRS // GROUPS
SOURCES = CHANS * GROUPS
F32 = jnp.float32
BF16 = jnp.bfloat16


def adjoint(matrix):
    re, im = matrix
    return ([re[0], re[2], re[1], re[3]], [-im[0], -im[2], -im[1], -im[3]])


def product(left, right):
    lr, li = left
    rr, ri = right
    out_re, out_im = [], []
    for row in range(2):
        for col in range(2):
            a = 2 * row
            out_re.append(lr[a] * rr[col] - li[a] * ri[col] + lr[a + 1] * rr[col + 2] - li[a + 1] * ri[col + 2])
            out_im.append(lr[a] * ri[col] + li[a] * rr[col] + lr[a + 1] * ri[col + 2] + li[a + 1] * rr[col + 2])
    return (out_re, out_im)


def normal(matrix):
    re, im = matrix
    return [
        re[0] ** 2 + im[0] ** 2 + re[1] ** 2 + im[1] ** 2,
        re[2] ** 2 + im[2] ** 2 + re[3] ** 2 + im[3] ** 2,
        re[0] * re[2] + im[0] * im[2] + re[1] * re[3] + im[1] * im[3],
        im[0] * re[2] - re[0] * im[2] + im[1] * re[3] - re[1] * im[3],
    ]


def two_parts(x):
    high = x.astype(BF16)
    low = (x - high.astype(F32)).astype(BF16)
    return jnp.concatenate([high, low], axis=0)


SMEM = pl.BlockSpec(memory_space=pltpu.SMEM)
VMEM = pl.BlockSpec(memory_space=pltpu.VMEM)

def call(kernel, outs, *args, scratch=(), fast=None, kinds=None, slow_outs=False, limit=12 << 20, name=None):
    fast = range(len(args)) if fast is None else fast
    args = [
        pltpu.with_memory_space_constraint(a, pltpu.MemorySpace.VMEM) if n in fast else a
        for n, a in enumerate(args)
    ]
    kind = jax.ShapeDtypeStruct if slow_outs else pltpu.VMEM
    many = isinstance(outs, list)
    kinds = kinds or [F32] * len(outs)
    return pl.pallas_call(
        kernel,
        out_shape=tuple(kind(o, t) for o, t in zip(outs, kinds)) if many else kind(outs, F32),
        in_specs=[SMEM if a.dtype == jnp.int32 and a.ndim == 1 else VMEM for a in args],
        out_specs=tuple(VMEM for _ in outs) if many else VMEM,
        scratch_shapes=list(scratch),
        compiler_params=pltpu.CompilerParams(vmem_limit_bytes=limit),
        name=name,
    )(*args)


def basis_of(channel, count):
    x = (2.0 * channel.astype(F32) + 1.0) / count - 1.0
    return [1.0 + 0.0 * x, x, 1.5 * x * x - 0.5, 2.5 * x * x * x - 1.5 * x]


def inverse_gram(count):
    x = (2.0 * np.arange(count) + 1.0) / count - 1.0
    basis = np.stack([np.ones_like(x), x, 1.5 * x * x - 0.5, 2.5 * x**3 - 1.5 * x], axis=1)
    return np.linalg.inv(basis.T @ basis)


def weights_of(basis, gram):
    return [sum(float(gram[j, i]) * basis[i] for i in range(POLY)) for j in range(POLY)]


def split(parts):
    return (parts[:4], parts[4:])


def flat(matrix):
    return matrix[0] + matrix[1]


def pack_kernel(gains_ref, coh_ref, vis_ref, pairs_ref, out_ref, sky):
    station = lax.broadcasted_iota(jnp.int32, (STATIONS, ROWS), 0)
    hot = [jnp.where(station == pairs_ref[i : i + 1, :], 1.0, 0.0) for i in range(2)]
    hot = jnp.concatenate(hot, axis=1).astype(BF16)
    rows = gains_ref[...].reshape(CHANS * 8 * DIRS, STATIONS)
    found = jnp.dot(two_parts(rows), hot, preferred_element_type=F32)
    found = found[: rows.shape[0]] + found[rows.shape[0] :]
    names = jnp.concatenate(
        [pairs_ref[0:2, :].astype(F32), jnp.zeros((6, ROWS), F32)],
        axis=0,
    )
    for c in range(CHANS):
        at = [found[(c * 8 + i) * DIRS : (c * 8 + i + 1) * DIRS] for i in range(8)]
        first = split([a[:, :ROWS] for a in at])
        second = split([a[:, ROWS:] for a in at])
        parts = [coh_ref[c, i].astype(F32) for i in range(8)]
        for i in range(8):
            sky[c, pl.ds(i * DIRS, DIRS), :] = parts[i]
        model = flat(product(product(first, split(parts)), adjoint(second)))
        rest = vis_ref[c] - jnp.concatenate([jnp.sum(m, axis=0, keepdims=True) for m in model], axis=0)
        for g in range(GROUPS):
            for d in range(PAIR):
                out_ref[c * GROUPS + g, pl.ds(d * 8, 8), :] = sky[c, pl.ds(d * GROUPS + g, 8, stride=DIRS), :]
            out_ref[c * GROUPS + g, pl.ds(16, 8), :] = rest
            out_ref[c * GROUPS + g, pl.ds(24, 8), :] = names


def own_kernel(count, index_ref, gains_ref, duals_ref, poly_ref, out_ref):
    freq, c, g = index_ref[0], index_ref[1], index_ref[2]
    basis = basis_of(freq * CHANS + c, count)
    sublane = lax.broadcasted_iota(jnp.int32, (DIRS, STATIONS), 0)
    for i in range(8):
        prior = basis[0] * poly_ref[0, i]
        for j in range(1, POLY):
            prior += basis[j] * poly_ref[j, i]
        for n, tile in enumerate((gains_ref[c, i], duals_ref[c, i], prior)):
            for d in range(PAIR):
                row = jnp.sum(jnp.where(sublane == d * GROUPS + g, tile, 0.0), axis=0, keepdims=True)
                for q in range(CUTS):
                    out_ref[n, pl.ds(i * 8 + q * PAIR + d, 1), :] = row[:, q * LANES : (q + 1) * LANES]


def looked_up(gains_ref, hot_ref, at_ref):
    rows = jnp.concatenate(
        [
            jnp.concatenate(
                [gains_ref[pl.ds(q * PAIR + d, 8, stride=8), :] for q in range(CUTS)], axis=1
            )
            for d in range(PAIR)
        ],
        axis=0,
    )
    found = jnp.dot(two_parts(rows), hot_ref[...], preferred_element_type=F32)
    found = found[:16] + found[16:]
    for b in range(2 * SOURCES):
        at_ref[pl.ds(b * 16, 16), :] = found[:, b * ROWS : (b + 1) * ROWS]


def ends(at_ref, d):
    first = [at_ref[pl.ds(d * 8 + i, SOURCES, stride=16), :] for i in range(8)]
    second = [at_ref[pl.ds(SOURCES * 16 + d * 8 + i, SOURCES, stride=16), :] for i in range(8)]
    return split(first), split(second)


def sky_of(rows_ref, d):
    return split([rows_ref[pl.ds(d * 8 + i, SOURCES, stride=32), :] for i in range(8)])


def summed(rest, rows_ref, at_ref, hot_ref, out_ref, terms, total_ref):
    half = SOURCES * 24
    for d in range(PAIR):
        first, second = ends(at_ref, d)
        sky = sky_of(rows_ref, d)
        left = product(first, sky)
        right = product(sky, adjoint(second))
        ahead = flat(product(rest, adjoint(right))) + normal(right)
        behind = flat(product(adjoint(rest), left)) + normal(adjoint(left))
        for i in range(12):
            terms[pl.ds(d * 12 + i, SOURCES, stride=24), :] = ahead[i]
            terms[pl.ds(half + d * 12 + i, SOURCES, stride=24), :] = behind[i]
    wide = jnp.concatenate([terms[pl.ds(b * 24, 24), :] for b in range(2 * SOURCES)], axis=1)
    total = lax.dot_general(
        two_parts(wide), hot_ref[...], (((1,), (1,)), ((), ())), preferred_element_type=F32
    )
    total = total[:24] + total[24:]
    for q in range(CUTS):
        total_ref[q] = total[:, q * LANES : (q + 1) * LANES]
    for q in range(CUTS):
        for d in range(PAIR):
            part = total_ref[q, pl.ds(d * 12, 12), :]
            for n in range(out_ref.shape[0]):
                out_ref[n, pl.ds(q * PAIR + d, 12, stride=8), :] = part


def model_of(rows_ref, at_ref):
    model = None
    for d in range(PAIR):
        first, second = ends(at_ref, d)
        part = flat(product(product(first, sky_of(rows_ref, d)), adjoint(second)))
        model = part if model is None else [a + b for a, b in zip(model, part)]
    return model


def start_kernel(rows_ref, own_ref, out_ref, hot_ref, model_ref, at, terms, total):
    station = lax.broadcasted_iota(jnp.int32, (STATIONS, ROWS), 0).astype(F32)
    for end in range(2):
        for n in range(SOURCES):
            name = rows_ref[pl.ds(n * 32 + 24 + end, 1), :]
            lanes = pl.ds((end * SOURCES + n) * ROWS, ROWS)
            hot_ref[:, lanes] = jnp.where(station == name, 1.0, 0.0).astype(BF16)
    looked_up(own_ref.at[0], hot_ref, at)
    rest = split([rows_ref[pl.ds(16 + i, SOURCES, stride=32), :] for i in range(8)])
    summed(rest, rows_ref, at, hot_ref, out_ref, terms, total)
    model = model_of(rows_ref, at)
    for i in range(8):
        model_ref[pl.ds(i * 8, 8), :] = model[i]


def stepped(arrived, gains_ref, own_ref, damping, put):
    total = []
    for i in range(12):
        value = arrived[0, pl.ds(i * 8, 8), :]
        for n in range(1, arrived.shape[0]):
            value = value + arrived[n, pl.ds(i * 8, 8), :]
        total.append(value)
    tile = lambda ref, i: ref[pl.ds(i * 8, 8), :]
    gains = [tile(gains_ref, i) for i in range(8)]
    way = [
        total[i] - tile(own_ref.at[1], i) - RHO * (gains[i] - tile(own_ref.at[2], i)) for i in range(8)
    ]
    top, bottom, cross_re, cross_im = total[8:]
    shift = damping * 0.5 * (top + bottom) + RHO
    upper = top + shift
    lower = bottom + shift
    scale = 1.0 / (upper * lower - cross_re * cross_re - cross_im * cross_im)
    zeros = jnp.zeros_like(scale)
    inverse = (
        [lower * scale, -cross_re * scale, -cross_re * scale, upper * scale],
        [zeros, -cross_im * scale, cross_im * scale, zeros],
    )
    step = flat(product(split(way), inverse))
    new = [gains[i] + step[i] for i in range(8)]
    for i in range(8):
        put[pl.ds(i * 8, 8), :] = new[i]
    return new


def middle_kernel(damping, arrived, own_ref, rows_ref, hot_ref, model_ref, out_ref, gains_ref, at_ref):
    stepped(arrived, own_ref.at[0], own_ref, damping, gains_ref)
    looked_up(gains_ref, hot_ref, at_ref)
    model = model_of(rows_ref, at_ref)
    for i in range(8):
        change = model_ref[pl.ds(i * 8, 8), :] - model[i]
        for n in range(out_ref.shape[0]):
            out_ref[n, pl.ds(i * 8, 8), :] = change


def second_kernel(arrived, rows_ref, hot_ref, at_ref, out_ref, terms, total):
    rest = []
    for i in range(8):
        value = rows_ref[pl.ds(16 + i, SOURCES, stride=32), :]
        for n in range(arrived.shape[0]):
            value = value + arrived[n, pl.ds(i * 8, 8), :]
        rest.append(value)
    summed(split(rest), rows_ref, at_ref, hot_ref, out_ref, terms, total)


def last_kernel(damping, count, gram, index_ref, arrived, gains_ref, own_ref, fit_ref, mine_ref, new):
    gains = stepped(arrived, gains_ref, own_ref, damping, new)
    freq, c, q = index_ref[0], index_ref[1], index_ref[3]
    weights = weights_of(basis_of(freq * CHANS + c, count), gram)

    def own_cut(tile):
        chosen = tile[:PAIR]
        for n in range(1, CUTS):
            chosen = jnp.where(q == n, tile[n * PAIR : (n + 1) * PAIR], chosen)
        return chosen

    mine_ref[...] = jnp.concatenate([own_cut(g) for g in gains], axis=0)
    mixed = jnp.concatenate(
        [own_cut(gains[i] + own_ref[1, pl.ds(i * 8, 8), :] / RHO) for i in range(8)], axis=0
    )
    for n in range(fit_ref.shape[0]):
        fit_ref[n] = weights[n % POLY] * mixed


def joined_kernel(arrived, gains_ref, out_ref):
    total = arrived[0]
    for n in range(1, arrived.shape[0]):
        total = total + arrived[n]
    gains = gains_ref[...]
    for n in range(out_ref.shape[0]):
        out_ref[n, pl.ds(0, 16), :] = gains
        out_ref[n, pl.ds(16, 16), :] = total


def end_kernel(count, index_ref, all_ref, other_ref, duals_ref, gains_out, duals_out, poly_out):
    freq = index_ref[0]
    core = freq % 2
    basis = [basis_of(freq * CHANS + c, count) for c in range(CHANS)]
    mine = [[jnp.where(core == 0, basis[c][j], basis[c][j + 2]) for j in range(2)] for c in range(CHANS)]
    his = [[jnp.where(core == 0, basis[c][j + 2], basis[c][j]) for j in range(2)] for c in range(CHANS)]

    def tile(ref, c, q, row, size):
        place = c * 16 + (q // 2) * 8 + q % 2
        return jnp.concatenate(
            [ref[pl.ds(place * size + row + d, GROUPS, stride=2 * size), :] for d in range(PAIR)], axis=0
        )

    for i in range(8):
        for q in range(CUTS):
            lanes = pl.ds(q * LANES, LANES)
            own = [tile(all_ref, c, q, 16 + i * PAIR, 32) for c in range(CHANS)]
            far = [tile(other_ref, c, q, i * PAIR, 16) for c in range(CHANS)]
            for j in range(2):
                poly_out[2 * core + j, i, :, lanes] = own[j]
                poly_out[2 - 2 * core + j, i, :, lanes] = far[j]
            for c in range(CHANS):
                gains = tile(all_ref, c, q, i * PAIR, 32)
                gains_out[c, i, :, lanes] = gains
                prior = mine[c][0] * own[0] + mine[c][1] * own[1] + his[c][0] * far[0] + his[c][1] * far[1]
                duals_out[c, i, :, lanes] = duals_ref[c, i, :, lanes] + RHO * (gains - prior)


def exchanged(x, axis):
    return lax.all_to_all(x, axis, split_axis=0, concat_axis=0, tiled=True)


TIMES = ("c", "r1", "g", "r0")


def shards(visibilities, coherencies, pairs, gains_start, duals_start, poly_start):
    freqs = lax.axis_size("freq")
    times = lax.axis_size(TIMES)
    count = CHANS * freqs
    index = jnp.stack(
        [lax.axis_index("freq"), lax.axis_index("c"), lax.axis_index("g"), lax.axis_index(("r1", "r0"))]
    ).astype(jnp.int32)
    sums_shape = (CUTS, 12 * 8, LANES)
    tiles = (64, LANES)
    share = (16, LANES)
    work = [pltpu.VMEM((2 * SOURCES * 24, ROWS), F32), pltpu.VMEM((CUTS, 24, LANES), F32)]

    sent = call(
        pack_kernel,
        (SOURCES, 32, ROWS),
        gains_start,
        coherencies,
        visibilities,
        pairs,
        fast=[],
        limit=60 << 20,
        scratch=[pltpu.VMEM((CHANS, 64, ROWS), F32)],
        name="pack",
    )
    own = call(
        functools.partial(own_kernel, count), (3, *tiles), index, gains_start, duals_start, poly_start, fast=[], name="own"
    )
    rows = exchanged(sent, ("c", "g")).reshape(SOURCES * 32, ROWS)
    sums, hot, model = call(
        start_kernel,
        [sums_shape, (STATIONS, 2 * SOURCES * ROWS), tiles],
        rows,
        own,
        kinds=[F32, BF16, F32],
        scratch=[pltpu.VMEM((2 * SOURCES * 16, ROWS), F32), *work],
        name="start",
    )
    sums = exchanged(sums, ("r1", "r0"))
    change, gains, at = call(
        functools.partial(middle_kernel, 12.0),
        [(GROUPS, *tiles), tiles, (2 * SOURCES * 16, ROWS)],
        sums,
        own,
        rows,
        hot,
        model,
        name="middle",
    )
    change = exchanged(change, "g")
    sums = call(second_kernel, sums_shape, change, rows, hot, at, scratch=work, name="second")
    sums = exchanged(sums, ("r1", "r0"))
    fits, mine = call(
        functools.partial(last_kernel, 6.0, count, inverse_gram(count)),
        [(freqs * CHANS, *share), share],
        index,
        sums,
        gains,
        own,
        fast=[1, 2, 3],
        scratch=[pltpu.VMEM(tiles, F32)],
        name="last",
    )
    fits = exchanged(fits, ("freq", "c"))
    copies = call(joined_kernel, (times, 32, LANES), fits, mine, name="joined")
    everything = exchanged(copies, TIMES)
    other = lax.ppermute(everything[:, 16:], "freq", [(i, i ^ 1) for i in range(freqs)])
    block = (CHANS, 8, DIRS, STATIONS)
    return call(
        functools.partial(end_kernel, count),
        [block, block, (POLY, 8, DIRS, STATIONS)],
        index,
        everything.reshape(times * 32, LANES),
        other.reshape(times * 16, LANES),
        duals_start,
        fast=[1, 2, 3],
        slow_outs=True,
        name="end",
    )


def solution(mesh):
    freqs = mesh.shape["freq"]
    fine = Mesh(mesh.devices.reshape(freqs, CHANS, 2, GROUPS, 2), ("freq", *TIMES))
    placed = (
        P("freq", None, TIMES),
        P("freq", None, None, TIMES),
        P(None, TIMES),
        P("freq", None, None, None),
        P("freq", None, None, None),
        P(),
    )
    return jax.shard_map(
        shards,
        mesh=fine,
        in_specs=placed,
        out_specs=(P("freq", None, None, None), P("freq", None, None, None), P()),
        check_vma=False,
    )
```

```python
import functools

import jax
import jax.numpy as jnp
import numpy as np
from jax import lax
from jax.experimental import pallas as pl
from jax.experimental.pallas import tpu as pltpu
from jax.sharding import Mesh
from jax.sharding import PartitionSpec as P

ITERS = 2
RHO = 16.0
CHANS = 2
DIRS = 8
STATIONS = 512
ROWS = 128
POLY = 4
LANES = 128
CUTS = STATIONS // LANES
GROUPS = 4
PAIR = DIRS // GROUPS
SOURCES = CHANS * GROUPS
F32 = jnp.float32
BF16 = jnp.bfloat16


def adjoint(matrix):
    re, im = matrix
    return ([re[0], re[2], re[1], re[3]], [-im[0], -im[2], -im[1], -im[3]])


def product(left, right):
    lr, li = left
    rr, ri = right
    out_re, out_im = [], []
    for row in range(2):
        for col in range(2):
            a = 2 * row
            out_re.append(lr[a] * rr[col] - li[a] * ri[col] + lr[a + 1] * rr[col + 2] - li[a + 1] * ri[col + 2])
            out_im.append(lr[a] * ri[col] + li[a] * rr[col] + lr[a + 1] * ri[col + 2] + li[a + 1] * rr[col + 2])
    return (out_re, out_im)


def normal(matrix):
    re, im = matrix
    return [
        re[0] ** 2 + im[0] ** 2 + re[1] ** 2 + im[1] ** 2,
        re[2] ** 2 + im[2] ** 2 + re[3] ** 2 + im[3] ** 2,
        re[0] * re[2] + im[0] * im[2] + re[1] * re[3] + im[1] * im[3],
        im[0] * re[2] - re[0] * im[2] + im[1] * re[3] - re[1] * im[3],
    ]


def two_parts(x):
    high = x.astype(BF16)
    low = (x - high.astype(F32)).astype(BF16)
    return jnp.concatenate([high, low], axis=0)


VMEM = pl.BlockSpec(memory_space=pltpu.VMEM)
HBM = pl.BlockSpec(memory_space=pltpu.HBM)


def in_vmem(x):
    return pltpu.with_memory_space_constraint(x, pltpu.MemorySpace.VMEM)


def call(kernel, outs, *args, scratch=(), fast=None, kinds=None, limit=12 << 20, name=None):
    fast = range(len(args)) if fast is None else fast
    args = [in_vmem(a) if n in fast else a for n, a in enumerate(args)]
    many = isinstance(outs, list)
    kinds = kinds or [F32] * len(outs)
    return pl.pallas_call(
        kernel,
        out_shape=tuple(pltpu.VMEM(o, t) for o, t in zip(outs, kinds)) if many else pltpu.VMEM(outs, F32),
        in_specs=[VMEM for _ in args],
        out_specs=tuple(VMEM for _ in outs) if many else VMEM,
        scratch_shapes=list(scratch),
        compiler_params=pltpu.CompilerParams(vmem_limit_bytes=limit),
        name=name,
    )(*args)


def basis_of(channel, count):
    x = (2.0 * channel.astype(F32) + 1.0) / count - 1.0
    return [1.0 + 0.0 * x, x, 1.5 * x * x - 0.5, 2.5 * x * x * x - 1.5 * x]


def inverse_gram(count):
    x = (2.0 * np.arange(count) + 1.0) / count - 1.0
    basis = np.stack([np.ones_like(x), x, 1.5 * x * x - 0.5, 2.5 * x**3 - 1.5 * x], axis=1)
    return np.linalg.inv(basis.T @ basis)


def weights_of(basis, gram):
    return [sum(float(gram[j, i]) * basis[i] for i in range(POLY)) for j in range(POLY)]


def split(parts):
    return (parts[:4], parts[4:])


def flat(matrix):
    return matrix[0] + matrix[1]


def pack_kernel(gains_ref, coh_ref, vis_ref, pairs_ref, out_ref, sky):
    station = lax.broadcasted_iota(jnp.int32, (STATIONS, ROWS), 0)
    hot = [jnp.where(station == pairs_ref[i : i + 1, :], 1.0, 0.0) for i in range(2)]
    hot = jnp.concatenate(hot, axis=1).astype(BF16)
    rows = gains_ref[...].reshape(CHANS * 8 * DIRS, STATIONS)
    found = jnp.dot(two_parts(rows), hot, preferred_element_type=F32)
    found = found[: rows.shape[0]] + found[rows.shape[0] :]
    names = jnp.concatenate(
        [pairs_ref[0:2, :].astype(F32), jnp.zeros((6, ROWS), F32)],
        axis=0,
    )
    for c in range(CHANS):
        at = [found[(c * 8 + i) * DIRS : (c * 8 + i + 1) * DIRS] for i in range(8)]
        first = split([a[:, :ROWS] for a in at])
        second = split([a[:, ROWS:] for a in at])
        parts = [coh_ref[c, i].astype(F32) for i in range(8)]
        for i in range(8):
            sky[c, pl.ds(i * DIRS, DIRS), :] = parts[i]
        model = flat(product(product(first, split(parts)), adjoint(second)))
        rest = vis_ref[c] - jnp.concatenate([jnp.sum(m, axis=0, keepdims=True) for m in model], axis=0)
        for g in range(GROUPS):
            for d in range(PAIR):
                out_ref[c * GROUPS + g, pl.ds(d * 8, 8), :] = sky[c, pl.ds(d * GROUPS + g, 8, stride=DIRS), :]
            out_ref[c * GROUPS + g, pl.ds(16, 8), :] = rest
            out_ref[c * GROUPS + g, pl.ds(24, 8), :] = names


def place_of():
    own = lax.axis_index("r1") * 2 + lax.axis_index("r0")
    return lax.axis_index("freq"), lax.axis_index("c"), lax.axis_index("g"), own


def own_kernel(count, gains_ref, duals_ref, poly_ref, out_ref, cut_ref):
    freq, c, g, own = place_of()
    basis = basis_of(freq * CHANS + c, count)
    sublane = lax.broadcasted_iota(jnp.int32, (DIRS, STATIONS), 0)
    for i in range(8):
        prior = basis[0] * poly_ref[0, i]
        for j in range(1, POLY):
            prior += basis[j] * poly_ref[j, i]
        for n, tile in enumerate((gains_ref[c, i], duals_ref[c, i], prior)):
            for d in range(PAIR):
                row = jnp.sum(jnp.where(sublane == d * GROUPS + g, tile, 0.0), axis=0, keepdims=True)
                parts = [row[:, q * LANES : (q + 1) * LANES] for q in range(CUTS)]
                chosen = parts[0]
                for q in range(CUTS):
                    out_ref[n, pl.ds(i * 8 + q * PAIR + d, 1), :] = parts[q]
                    chosen = jnp.where(own == q, parts[q], chosen)
                cut_ref[n, pl.ds(d * 8 + i, 1), :] = chosen


def looked_up(gains_ref, hot_ref, at_ref):
    rows = jnp.concatenate(
        [
            jnp.concatenate(
                [gains_ref[pl.ds(q * PAIR + d, 8, stride=8), :] for q in range(CUTS)], axis=1
            )
            for d in range(PAIR)
        ],
        axis=0,
    )
    found = jnp.dot(two_parts(rows), hot_ref[...], preferred_element_type=F32)
    found = found[:16] + found[16:]
    for b in range(2 * SOURCES):
        at_ref[pl.ds(b * 16, 16), :] = found[:, b * ROWS : (b + 1) * ROWS]


def ends(at_ref, d):
    first = [at_ref[pl.ds(d * 8 + i, SOURCES, stride=16), :] for i in range(8)]
    second = [at_ref[pl.ds(SOURCES * 16 + d * 8 + i, SOURCES, stride=16), :] for i in range(8)]
    return split(first), split(second)


def sky_of(rows_ref, d):
    return split([rows_ref[pl.ds(d * 8 + i, SOURCES, stride=32), :] for i in range(8)])


def summed(rest, rows_ref, at_ref, hot_ref, terms, total_ref):
    half = SOURCES * 24
    for d in range(PAIR):
        first, second = ends(at_ref, d)
        sky = sky_of(rows_ref, d)
        left = product(first, sky)
        right = product(sky, adjoint(second))
        ahead = flat(product(rest, adjoint(right))) + normal(right)
        behind = flat(product(adjoint(rest), left)) + normal(adjoint(left))
        for i in range(12):
            terms[pl.ds(d * 12 + i, SOURCES, stride=24), :] = ahead[i]
            terms[pl.ds(half + d * 12 + i, SOURCES, stride=24), :] = behind[i]
    wide = jnp.concatenate([terms[pl.ds(b * 24, 24), :] for b in range(2 * SOURCES)], axis=1)
    total = lax.dot_general(
        two_parts(wide), hot_ref[...], (((1,), (1,)), ((), ())), preferred_element_type=F32
    )
    total = total[:24] + total[24:]
    for q in range(CUTS):
        total_ref[q] = total[:, q * LANES : (q + 1) * LANES]


def model_of(rows_ref, at_ref):
    model = None
    for d in range(PAIR):
        first, second = ends(at_ref, d)
        part = flat(product(product(first, sky_of(rows_ref, d)), adjoint(second)))
        model = part if model is None else [a + b for a, b in zip(model, part)]
    return model


def start_kernel(rows_ref, own_ref, out_ref, hot_ref, model_ref, at, terms, total):
    station = lax.broadcasted_iota(jnp.int32, (STATIONS, ROWS), 0).astype(F32)
    for end in range(2):
        for n in range(SOURCES):
            name = rows_ref[pl.ds(n * 32 + 24 + end, 1), :]
            lanes = pl.ds((end * SOURCES + n) * ROWS, ROWS)
            hot_ref[:, lanes] = jnp.where(station == name, 1.0, 0.0).astype(BF16)
    looked_up(own_ref.at[0], hot_ref, at)
    rest = split([rows_ref[pl.ds(16 + i, SOURCES, stride=32), :] for i in range(8)])
    summed(rest, rows_ref, at, hot_ref, terms, total)
    for q in range(CUTS):
        for d in range(PAIR):
            part = total[q, pl.ds(d * 12, 12), :]
            for n in range(out_ref.shape[0]):
                out_ref[n, pl.ds(q * PAIR + d, 12, stride=8), :] = part
    model = model_of(rows_ref, at)
    for i in range(8):
        model_ref[pl.ds(i * 8, 8), :] = model[i]


def stepped(total, gains, duals, prior, damping):
    way = [total[i] - duals[i] - RHO * (gains[i] - prior[i]) for i in range(8)]
    top, bottom, cross_re, cross_im = total[8:]
    shift = damping * 0.5 * (top + bottom) + RHO
    upper = top + shift
    lower = bottom + shift
    scale = 1.0 / (upper * lower - cross_re * cross_re - cross_im * cross_im)
    zeros = jnp.zeros_like(scale)
    inverse = (
        [lower * scale, -cross_re * scale, -cross_re * scale, upper * scale],
        [zeros, -cross_im * scale, cross_im * scale, zeros],
    )
    step = flat(product(split(way), inverse))
    return [gains[i] + step[i] for i in range(8)]


def middle_kernel(
    damping, arrived, own_ref, rows_ref, hot_ref, model_ref, out_ref, cut_ref, at_ref, gains_ref
):
    own = place_of()[3]
    total = []
    for i in range(12):
        value = arrived[0, pl.ds(i * 8, 8), :]
        for n in range(1, arrived.shape[0]):
            value = value + arrived[n, pl.ds(i * 8, 8), :]
        total.append(value)
    start = [[own_ref[n, pl.ds(i * 8, 8), :] for i in range(8)] for n in range(3)]
    new = stepped(total, *start, damping)
    for i in range(8):
        gains_ref[pl.ds(i * 8, 8), :] = new[i]
        chosen = new[i][:PAIR]
        for q in range(1, CUTS):
            chosen = jnp.where(own == q, new[i][q * PAIR : (q + 1) * PAIR], chosen)
        cut_ref[pl.ds(i, PAIR, stride=8), :] = chosen
    looked_up(gains_ref, hot_ref, at_ref)
    model = model_of(rows_ref, at_ref)
    for i in range(8):
        change = model_ref[pl.ds(i * 8, 8), :] - model[i]
        for n in range(out_ref.shape[0]):
            out_ref[n, pl.ds(i * 8, 8), :] = change


def second_kernel(arrived, rows_ref, hot_ref, at_ref, out_ref, terms):
    rest = []
    for i in range(8):
        value = rows_ref[pl.ds(16 + i, SOURCES, stride=32), :]
        for n in range(arrived.shape[0]):
            value = value + arrived[n, pl.ds(i * 8, 8), :]
        rest.append(value)
    summed(split(rest), rows_ref, at_ref, hot_ref, terms, out_ref)


def last_kernel(damping, count, gram, arrived, gains_ref, own_ref, fit_ref, mine_ref, total_ref):
    value = arrived[0]
    for n in range(1, arrived.shape[0]):
        value = value + arrived[n]
    total_ref[...] = value
    total = [total_ref[pl.ds(i, PAIR, stride=12), :] for i in range(12)]
    gains = [gains_ref[pl.ds(i, PAIR, stride=8), :] for i in range(8)]
    duals, prior = [[own_ref[n, pl.ds(i, PAIR, stride=8), :] for i in range(8)] for n in (1, 2)]
    new = stepped(total, gains, duals, prior, damping)
    for i in range(8):
        mine_ref[pl.ds(i, PAIR, stride=8), :] = new[i]
    freq, c, _, _ = place_of()
    weights = weights_of(basis_of(freq * CHANS + c, count), gram)
    mixed = mine_ref[...] + own_ref[1] / RHO
    for n in range(fit_ref.shape[0]):
        fit_ref[n] = weights[n % POLY] * mixed


def joined_kernel(arrived, gains_ref, out_ref):
    total = arrived[0]
    for n in range(1, arrived.shape[0]):
        total = total + arrived[n]
    gains = gains_ref[...]
    for n in range(out_ref.shape[0]):
        out_ref[n, pl.ds(0, 16), :] = gains
        out_ref[n, pl.ds(16, 16), :] = total


def tile_of(ref, c, q, row, size):
    place = c * 16 + (q // 2) * 8 + q % 2
    return jnp.concatenate(
        [ref[pl.ds(place * size + row + d * 8, GROUPS, stride=2 * size), :] for d in range(PAIR)], axis=0
    )


def near_kernel(count, all_ref, duals_ref, gains_out, poly_out, part_ref, gains, poly, sems):
    freq = lax.axis_index("freq")
    core = freq % 2
    basis = [basis_of(freq * CHANS + c, count) for c in range(CHANS)]
    mine = [[jnp.where(core == 0, basis[c][j], basis[c][j + 2]) for j in range(2)] for c in range(CHANS)]
    to_gains = pltpu.make_async_copy(gains, gains_out, sems.at[0])
    to_poly = pltpu.make_async_copy(poly, poly_out.at[pl.ds(2 * core, 2)], sems.at[1])
    for i in range(8):
        for q in range(CUTS):
            for c in range(CHANS):
                gains[c, i, :, q * LANES : (q + 1) * LANES] = tile_of(all_ref, c, q, i, 32)
    to_gains.start()
    for i in range(8):
        for q in range(CUTS):
            for j in range(2):
                poly[j, i, :, q * LANES : (q + 1) * LANES] = tile_of(all_ref, j, q, 16 + i, 32)
    to_poly.start()
    for c in range(CHANS):
        for i in range(8):
            prior = mine[c][0] * poly[0, i] + mine[c][1] * poly[1, i]
            part_ref[c, i] = duals_ref[c, i] + RHO * (gains[c, i] - prior)
    to_gains.wait()
    to_poly.wait()


def far_kernel(count, other_ref, part_ref, half_ref, duals_out, poly_out, duals, poly, sems):
    del half_ref
    freq = lax.axis_index("freq")
    core = freq % 2
    basis = [basis_of(freq * CHANS + c, count) for c in range(CHANS)]
    his = [[jnp.where(core == 0, basis[c][j + 2], basis[c][j]) for j in range(2)] for c in range(CHANS)]
    to_duals = pltpu.make_async_copy(duals, duals_out, sems.at[0])
    to_poly = pltpu.make_async_copy(poly, poly_out.at[pl.ds(2 - 2 * core, 2)], sems.at[1])
    for i in range(8):
        for q in range(CUTS):
            for j in range(2):
                poly[j, i, :, q * LANES : (q + 1) * LANES] = tile_of(other_ref, j, q, i, 16)
    to_poly.start()
    for c in range(CHANS):
        for i in range(8):
            duals[c, i] = part_ref[c, i] - RHO * (his[c][0] * poly[0, i] + his[c][1] * poly[1, i])
    to_duals.start()
    to_poly.wait()
    to_duals.wait()


def exchanged(x, axis):
    return lax.all_to_all(x, axis, split_axis=0, concat_axis=0, tiled=True)


TIMES = ("c", "r1", "g", "r0")


def shards(visibilities, coherencies, pairs, gains_start, duals_start, poly_start):
    freqs = lax.axis_size("freq")
    times = lax.axis_size(TIMES)
    count = CHANS * freqs
    sums_shape = (CUTS, 12 * 8, LANES)
    tiles = (64, LANES)
    share = (16, LANES)
    work = pltpu.VMEM((2 * SOURCES * 24, ROWS), F32)
    quarters = (CUTS, 24, LANES)

    sent = call(
        pack_kernel,
        (SOURCES, 32, ROWS),
        gains_start,
        coherencies,
        visibilities,
        pairs,
        fast=[],
        limit=60 << 20,
        scratch=[pltpu.VMEM((CHANS, 64, ROWS), F32)],
        name="pack",
    )
    own, cut = call(
        functools.partial(own_kernel, count),
        [(3, *tiles), (3, *share)],
        gains_start,
        duals_start,
        poly_start,
        fast=[],
        limit=60 << 20,
        name="own",
    )
    rows = exchanged(sent, ("c", "g")).reshape(SOURCES * 32, ROWS)
    sums, hot, model = call(
        start_kernel,
        [sums_shape, (STATIONS, 2 * SOURCES * ROWS), tiles],
        rows,
        own,
        kinds=[F32, BF16, F32],
        scratch=[pltpu.VMEM((2 * SOURCES * 16, ROWS), F32), work, pltpu.VMEM(quarters, F32)],
        name="start",
    )
    sums = exchanged(sums, ("r1", "r0"))
    change, gains, at = call(
        functools.partial(middle_kernel, 12.0),
        [(GROUPS, *tiles), share, (2 * SOURCES * 16, ROWS)],
        sums,
        own,
        rows,
        hot,
        model,
        scratch=[pltpu.VMEM(tiles, F32)],
        name="middle",
    )
    change = exchanged(change, "g")
    sums = call(second_kernel, quarters, change, rows, hot, at, scratch=[work], name="second")
    sums = exchanged(sums, ("r1", "r0"))
    fits, mine = call(
        functools.partial(last_kernel, 6.0, count, inverse_gram(count)),
        [(freqs * CHANS, *share), share],
        sums,
        gains,
        cut,
        scratch=[pltpu.VMEM((24, LANES), F32)],
        name="last",
    )
    fits = exchanged(fits, ("freq", "c"))
    copies = call(joined_kernel, (times, 32, LANES), fits, mine, name="joined")
    everything = exchanged(copies, TIMES)
    other = lax.ppermute(everything[:, 16:], "freq", [(i, i ^ 1) for i in range(freqs)])
    block = (CHANS, 8, DIRS, STATIONS)
    held = [pltpu.VMEM(block, F32), pltpu.VMEM(block, F32), pltpu.SemaphoreType.DMA((2,))]
    full = (POLY, 8, DIRS, STATIONS)
    everything = in_vmem(everything.reshape(times * 32, LANES))
    gains, half, part = pl.pallas_call(
        functools.partial(near_kernel, count),
        out_shape=(pltpu.HBM(block, F32), pltpu.HBM(full, F32), pltpu.VMEM(block, F32)),
        in_specs=[VMEM, VMEM],
        out_specs=(HBM, HBM, VMEM),
        scratch_shapes=held,
        compiler_params=pltpu.CompilerParams(vmem_limit_bytes=12 << 20),
        cost_estimate=pl.CostEstimate(flops=1000000, bytes_accessed=2000000, transcendentals=0),
        name="near",
    )(everything, in_vmem(duals_start))
    duals, polynomial = pl.pallas_call(
        functools.partial(far_kernel, count),
        out_shape=(pltpu.HBM(block, F32), pltpu.HBM(full, F32)),
        in_specs=[VMEM, VMEM, HBM],
        out_specs=(HBM, HBM),
        input_output_aliases={2: 1},
        scratch_shapes=held,
        compiler_params=pltpu.CompilerParams(vmem_limit_bytes=12 << 20),
        name="far",
    )(in_vmem(other.reshape(times * 16, LANES)), part, half)
    return (gains, duals, polynomial)


def solution(mesh):
    freqs = mesh.shape["freq"]
    fine = Mesh(mesh.devices.reshape(freqs, CHANS, 2, GROUPS, 2), ("freq", *TIMES))
    placed = (
        P("freq", None, TIMES),
        P("freq", None, None, TIMES),
        P(None, TIMES),
        P("freq", None, None, None),
        P("freq", None, None, None),
        P(),
    )
    return jax.shard_map(
        shards,
        mesh=fine,
        in_specs=placed,
        out_specs=(P("freq", None, None, None), P("freq", None, None, None), P()),
        check_vma=False,
    )
```

```python
import functools

import jax
import jax.numpy as jnp
import numpy as np
from jax import lax
from jax.experimental import pallas as pl
from jax.experimental.pallas import tpu as pltpu
from jax.sharding import Mesh
from jax.sharding import PartitionSpec as P

ITERS = 2
RHO = 16.0
CHANS = 2
DIRS = 8
STATIONS = 512
ROWS = 128
POLY = 4
LANES = 128
CUTS = STATIONS // LANES
GROUPS = 4
PAIR = DIRS // GROUPS
SOURCES = CHANS * GROUPS
F32 = jnp.float32
BF16 = jnp.bfloat16


def adjoint(matrix):
    re, im = matrix
    return ([re[0], re[2], re[1], re[3]], [-im[0], -im[2], -im[1], -im[3]])


def product(left, right):
    lr, li = left
    rr, ri = right
    out_re, out_im = [], []
    for row in range(2):
        for col in range(2):
            a = 2 * row
            out_re.append(lr[a] * rr[col] - li[a] * ri[col] + lr[a + 1] * rr[col + 2] - li[a + 1] * ri[col + 2])
            out_im.append(lr[a] * ri[col] + li[a] * rr[col] + lr[a + 1] * ri[col + 2] + li[a + 1] * rr[col + 2])
    return (out_re, out_im)


def normal(matrix):
    re, im = matrix
    return [
        re[0] ** 2 + im[0] ** 2 + re[1] ** 2 + im[1] ** 2,
        re[2] ** 2 + im[2] ** 2 + re[3] ** 2 + im[3] ** 2,
        re[0] * re[2] + im[0] * im[2] + re[1] * re[3] + im[1] * im[3],
        im[0] * re[2] - re[0] * im[2] + im[1] * re[3] - re[1] * im[3],
    ]


def two_parts(x):
    high = x.astype(BF16)
    low = (x - high.astype(F32)).astype(BF16)
    return jnp.concatenate([high, low], axis=0)


VMEM = pl.BlockSpec(memory_space=pltpu.VMEM)
HBM = pl.BlockSpec(memory_space=pltpu.HBM)


def in_vmem(x):
    return pltpu.with_memory_space_constraint(x, pltpu.MemorySpace.VMEM)


def call(kernel, outs, *args, scratch=(), fast=None, kinds=None, limit=12 << 20, name=None):
    fast = range(len(args)) if fast is None else fast
    args = [in_vmem(a) if n in fast else a for n, a in enumerate(args)]
    many = isinstance(outs, list)
    kinds = kinds or [F32] * len(outs)
    return pl.pallas_call(
        kernel,
        out_shape=tuple(pltpu.VMEM(o, t) for o, t in zip(outs, kinds)) if many else pltpu.VMEM(outs, F32),
        in_specs=[VMEM for _ in args],
        out_specs=tuple(VMEM for _ in outs) if many else VMEM,
        scratch_shapes=list(scratch),
        compiler_params=pltpu.CompilerParams(vmem_limit_bytes=limit),
        name=name,
    )(*args)


def basis_of(channel, count):
    x = (2.0 * channel.astype(F32) + 1.0) / count - 1.0
    return [1.0 + 0.0 * x, x, 1.5 * x * x - 0.5, 2.5 * x * x * x - 1.5 * x]


def fit_weights(count):
    x = (2.0 * np.arange(count) + 1.0) / count - 1.0
    basis = np.stack([np.ones_like(x), x, 1.5 * x * x - 0.5, 2.5 * x**3 - 1.5 * x], axis=1)
    return np.linalg.solve(basis.T @ basis, basis.T)


def split(parts):
    return (parts[:4], parts[4:])


def flat(matrix):
    return matrix[0] + matrix[1]


def pack_kernel(gains_ref, coh_ref, vis_ref, pairs_ref, out_ref, sky):
    station = lax.broadcasted_iota(jnp.int32, (STATIONS, ROWS), 0)
    hot = [jnp.where(station == pairs_ref[i : i + 1, :], 1.0, 0.0) for i in range(2)]
    hot = jnp.concatenate(hot, axis=1).astype(BF16)
    rows = gains_ref[...].reshape(CHANS * 8 * DIRS, STATIONS)
    found = jnp.dot(two_parts(rows), hot, preferred_element_type=F32)
    found = found[: rows.shape[0]] + found[rows.shape[0] :]
    names = jnp.concatenate(
        [pairs_ref[0:2, :].astype(F32), jnp.zeros((6, ROWS), F32)],
        axis=0,
    )
    for c in range(CHANS):
        at = [found[(c * 8 + i) * DIRS : (c * 8 + i + 1) * DIRS] for i in range(8)]
        first = split([a[:, :ROWS] for a in at])
        second = split([a[:, ROWS:] for a in at])
        parts = [coh_ref[c, i].astype(F32) for i in range(8)]
        for i in range(8):
            sky[c, pl.ds(i * DIRS, DIRS), :] = parts[i]
        model = flat(product(product(first, split(parts)), adjoint(second)))
        rest = vis_ref[c] - jnp.concatenate([jnp.sum(m, axis=0, keepdims=True) for m in model], axis=0)
        for g in range(GROUPS):
            for d in range(PAIR):
                out_ref[c * GROUPS + g, pl.ds(d * 8, 8), :] = sky[c, pl.ds(d * GROUPS + g, 8, stride=DIRS), :]
            out_ref[c * GROUPS + g, pl.ds(16, 8), :] = rest
            out_ref[c * GROUPS + g, pl.ds(24, 8), :] = names


def place_of():
    own = lax.axis_index("r1") * 2 + lax.axis_index("r0")
    return lax.axis_index("freq"), lax.axis_index("c"), lax.axis_index("g"), own


def own_kernel(count, gains_ref, duals_ref, poly_ref, out_ref, cut_ref):
    freq, c, g, own = place_of()
    basis = basis_of(freq * CHANS + c, count)
    sublane = lax.broadcasted_iota(jnp.int32, (DIRS, STATIONS), 0)
    for i in range(8):
        prior = basis[0] * poly_ref[0, i]
        for j in range(1, POLY):
            prior += basis[j] * poly_ref[j, i]
        for n, tile in enumerate((gains_ref[c, i], duals_ref[c, i], prior)):
            for d in range(PAIR):
                row = jnp.sum(jnp.where(sublane == d * GROUPS + g, tile, 0.0), axis=0, keepdims=True)
                parts = [row[:, q * LANES : (q + 1) * LANES] for q in range(CUTS)]
                chosen = parts[0]
                for q in range(CUTS):
                    out_ref[n, pl.ds(i * 8 + q * PAIR + d, 1), :] = parts[q]
                    chosen = jnp.where(own == q, parts[q], chosen)
                cut_ref[n, pl.ds(d * 8 + i, 1), :] = chosen


def looked_up(gains_ref, hot_ref, at_ref):
    rows = jnp.concatenate(
        [
            jnp.concatenate(
                [gains_ref[pl.ds(q * PAIR + d, 8, stride=8), :] for q in range(CUTS)], axis=1
            )
            for d in range(PAIR)
        ],
        axis=0,
    )
    found = jnp.dot(two_parts(rows), hot_ref[...], preferred_element_type=F32)
    found = found[:16] + found[16:]
    for b in range(2 * SOURCES):
        at_ref[pl.ds(b * 16, 16), :] = found[:, b * ROWS : (b + 1) * ROWS]


def ends(at_ref, d):
    first = [at_ref[pl.ds(d * 8 + i, SOURCES, stride=16), :] for i in range(8)]
    second = [at_ref[pl.ds(SOURCES * 16 + d * 8 + i, SOURCES, stride=16), :] for i in range(8)]
    return split(first), split(second)


def sky_of(rows_ref, d):
    return split([rows_ref[pl.ds(d * 8 + i, SOURCES, stride=32), :] for i in range(8)])


def summed(rest, rows_ref, at_ref, hot_ref, terms, total_ref):
    half = SOURCES * 24
    for d in range(PAIR):
        first, second = ends(at_ref, d)
        sky = sky_of(rows_ref, d)
        left = product(first, sky)
        right = product(sky, adjoint(second))
        ahead = flat(product(rest, adjoint(right))) + normal(right)
        behind = flat(product(adjoint(rest), left)) + normal(adjoint(left))
        for i in range(12):
            terms[pl.ds(d * 12 + i, SOURCES, stride=24), :] = ahead[i]
            terms[pl.ds(half + d * 12 + i, SOURCES, stride=24), :] = behind[i]
    wide = jnp.concatenate([terms[pl.ds(b * 24, 24), :] for b in range(2 * SOURCES)], axis=1)
    total = lax.dot_general(
        two_parts(wide), hot_ref[...], (((1,), (1,)), ((), ())), preferred_element_type=F32
    )
    total = total[:24] + total[24:]
    for q in range(CUTS):
        total_ref[q] = total[:, q * LANES : (q + 1) * LANES]


def model_of(rows_ref, at_ref):
    model = None
    for d in range(PAIR):
        first, second = ends(at_ref, d)
        part = flat(product(product(first, sky_of(rows_ref, d)), adjoint(second)))
        model = part if model is None else [a + b for a, b in zip(model, part)]
    return model


def start_kernel(rows_ref, own_ref, out_ref, hot_ref, model_ref, at, terms, total):
    station = lax.broadcasted_iota(jnp.int32, (STATIONS, ROWS), 0).astype(F32)
    for end in range(2):
        for n in range(SOURCES):
            name = rows_ref[pl.ds(n * 32 + 24 + end, 1), :]
            lanes = pl.ds((end * SOURCES + n) * ROWS, ROWS)
            hot_ref[:, lanes] = jnp.where(station == name, 1.0, 0.0).astype(BF16)
    looked_up(own_ref.at[0], hot_ref, at)
    rest = split([rows_ref[pl.ds(16 + i, SOURCES, stride=32), :] for i in range(8)])
    summed(rest, rows_ref, at, hot_ref, terms, total)
    for q in range(CUTS):
        for d in range(PAIR):
            part = total[q, pl.ds(d * 12, 12), :]
            for n in range(out_ref.shape[0]):
                out_ref[n, pl.ds(q * PAIR + d, 12, stride=8), :] = part
    model = model_of(rows_ref, at)
    for i in range(8):
        model_ref[pl.ds(i * 8, 8), :] = model[i]


def stepped(total, gains, duals, prior, damping):
    way = [total[i] - duals[i] - RHO * (gains[i] - prior[i]) for i in range(8)]
    top, bottom, cross_re, cross_im = total[8:]
    shift = damping * 0.5 * (top + bottom) + RHO
    upper = top + shift
    lower = bottom + shift
    scale = 1.0 / (upper * lower - cross_re * cross_re - cross_im * cross_im)
    zeros = jnp.zeros_like(scale)
    inverse = (
        [lower * scale, -cross_re * scale, -cross_re * scale, upper * scale],
        [zeros, -cross_im * scale, cross_im * scale, zeros],
    )
    step = flat(product(split(way), inverse))
    return [gains[i] + step[i] for i in range(8)]


def middle_kernel(
    damping, arrived, own_ref, rows_ref, hot_ref, model_ref, out_ref, cut_ref, at_ref, gains_ref
):
    own = place_of()[3]
    total = []
    for i in range(12):
        value = arrived[0, pl.ds(i * 8, 8), :]
        for n in range(1, arrived.shape[0]):
            value = value + arrived[n, pl.ds(i * 8, 8), :]
        total.append(value)
    start = [[own_ref[n, pl.ds(i * 8, 8), :] for i in range(8)] for n in range(3)]
    new = stepped(total, *start, damping)
    for i in range(8):
        gains_ref[pl.ds(i * 8, 8), :] = new[i]
        chosen = new[i][:PAIR]
        for q in range(1, CUTS):
            chosen = jnp.where(own == q, new[i][q * PAIR : (q + 1) * PAIR], chosen)
        cut_ref[pl.ds(i, PAIR, stride=8), :] = chosen
    looked_up(gains_ref, hot_ref, at_ref)
    model = model_of(rows_ref, at_ref)
    for i in range(8):
        change = model_ref[pl.ds(i * 8, 8), :] - model[i]
        for n in range(out_ref.shape[0]):
            out_ref[n, pl.ds(i * 8, 8), :] = change


def second_kernel(arrived, rows_ref, hot_ref, at_ref, out_ref, terms):
    rest = []
    for i in range(8):
        value = rows_ref[pl.ds(16 + i, SOURCES, stride=32), :]
        for n in range(arrived.shape[0]):
            value = value + arrived[n, pl.ds(i * 8, 8), :]
        rest.append(value)
    summed(split(rest), rows_ref, at_ref, hot_ref, terms, out_ref)


def last_kernel(damping, arrived, gains_ref, own_ref, out_ref, total_ref, new_ref):
    value = arrived[0]
    for n in range(1, arrived.shape[0]):
        value = value + arrived[n]
    total_ref[...] = value
    total = [total_ref[pl.ds(i, PAIR, stride=12), :] for i in range(12)]
    gains = [gains_ref[pl.ds(i, PAIR, stride=8), :] for i in range(8)]
    duals, prior = [[own_ref[n, pl.ds(i, PAIR, stride=8), :] for i in range(8)] for n in (1, 2)]
    new = stepped(total, gains, duals, prior, damping)
    for i in range(8):
        new_ref[pl.ds(i, PAIR, stride=8), :] = new[i]
    mixed = new_ref[...] + own_ref[1] / RHO
    for n in range(out_ref.shape[0]):
        out_ref[n] = mixed


def joined_kernel(weights, arrived, out_ref):
    freq = lax.axis_index("freq")
    first = freq % 2 == 0
    parts = [arrived[freq * CHANS + c] for c in range(CHANS)]
    mixed = [arrived[n] for n in range(arrived.shape[0])]
    for j in range(2):
        total = None
        for n, value in enumerate(mixed):
            weight = jnp.where(first, float(weights[j, n]), float(weights[j + 2, n]))
            total = weight * value if total is None else total + weight * value
        parts.append(total)
    for n in range(out_ref.shape[0]):
        for k, part in enumerate(parts):
            out_ref[n, pl.ds(k * 16, 16), :] = part


def tile_of(ref, q, row, size):
    place = (q // 2) * 8 + q % 2
    return jnp.concatenate(
        [ref[pl.ds(place * size + row + d * 8, GROUPS, stride=2 * size), :] for d in range(PAIR)], axis=0
    )


def sides(count):
    freq = lax.axis_index("freq")
    core = freq % 2
    basis = [basis_of(freq * CHANS + c, count) for c in range(CHANS)]
    mine = [[jnp.where(core == 0, b[j], b[j + 2]) for j in range(2)] for b in basis]
    his = [[jnp.where(core == 0, b[j + 2], b[j]) for j in range(2)] for b in basis]
    return core, mine, his


def near_kernel(count, all_ref, duals_ref, gains_out, poly_out, part_ref, gains, poly, sems):
    core, mine, _ = sides(count)
    to_gains = pltpu.make_async_copy(gains, gains_out, sems.at[0])
    to_poly = pltpu.make_async_copy(poly, poly_out.at[pl.ds(2 * core, 2)], sems.at[1])
    for i in range(8):
        for q in range(CUTS):
            lanes = slice(q * LANES, (q + 1) * LANES)
            for j in range(2):
                poly[j, i, :, lanes] = tile_of(all_ref, q, 32 + j * 16 + i, 64)
    to_poly.start()
    for c in range(CHANS):
        for i in range(8):
            mixed = jnp.concatenate([tile_of(all_ref, q, c * 16 + i, 64) for q in range(CUTS)], axis=1)
            gains[c, i] = mixed - duals_ref[c, i] / RHO
            part_ref[c, i] = RHO * (mixed - (mine[c][0] * poly[0, i] + mine[c][1] * poly[1, i]))
    to_gains.start()
    to_poly.wait()
    to_gains.wait()


def far_kernel(count, other_ref, part_ref, half_ref, duals_out, poly_out, duals, poly, sems):
    del half_ref
    core, _, his = sides(count)
    to_duals = pltpu.make_async_copy(duals, duals_out, sems.at[0])
    to_poly = pltpu.make_async_copy(poly, poly_out.at[pl.ds(2 - 2 * core, 2)], sems.at[1])
    for i in range(8):
        for q in range(CUTS):
            for j in range(2):
                poly[j, i, :, q * LANES : (q + 1) * LANES] = tile_of(other_ref, q, j * 16 + i, 32)
    to_poly.start()
    for c in range(CHANS):
        for i in range(8):
            duals[c, i] = part_ref[c, i] - RHO * (his[c][0] * poly[0, i] + his[c][1] * poly[1, i])
    to_duals.start()
    to_poly.wait()
    to_duals.wait()


def exchanged(x, axis):
    return lax.all_to_all(x, axis, split_axis=0, concat_axis=0, tiled=True)


TIMES = ("c", "r1", "g", "r0")


def shards(visibilities, coherencies, pairs, gains_start, duals_start, poly_start):
    freqs = lax.axis_size("freq")
    times = lax.axis_size(TIMES)
    count = CHANS * freqs
    sums_shape = (CUTS, 12 * 8, LANES)
    tiles = (64, LANES)
    share = (16, LANES)
    work = pltpu.VMEM((2 * SOURCES * 24, ROWS), F32)
    quarters = (CUTS, 24, LANES)

    sent = call(
        pack_kernel,
        (SOURCES, 32, ROWS),
        gains_start,
        coherencies,
        visibilities,
        pairs,
        fast=[],
        limit=60 << 20,
        scratch=[pltpu.VMEM((CHANS, 64, ROWS), F32)],
        name="pack",
    )
    own, cut = call(
        functools.partial(own_kernel, count),
        [(3, *tiles), (3, *share)],
        gains_start,
        duals_start,
        poly_start,
        fast=[],
        limit=60 << 20,
        name="own",
    )
    rows = exchanged(sent, ("c", "g")).reshape(SOURCES * 32, ROWS)
    sums, hot, model = call(
        start_kernel,
        [sums_shape, (STATIONS, 2 * SOURCES * ROWS), tiles],
        rows,
        own,
        kinds=[F32, BF16, F32],
        scratch=[pltpu.VMEM((2 * SOURCES * 16, ROWS), F32), work, pltpu.VMEM(quarters, F32)],
        name="start",
    )
    sums = exchanged(sums, ("r1", "r0"))
    change, gains, at = call(
        functools.partial(middle_kernel, 12.0),
        [(GROUPS, *tiles), share, (2 * SOURCES * 16, ROWS)],
        sums,
        own,
        rows,
        hot,
        model,
        scratch=[pltpu.VMEM(tiles, F32)],
        name="middle",
    )
    change = exchanged(change, "g")
    sums = call(second_kernel, quarters, change, rows, hot, at, scratch=[work], name="second")
    sums = exchanged(sums, ("r1", "r0"))
    mixed = call(
        functools.partial(last_kernel, 6.0),
        (freqs * CHANS, *share),
        sums,
        gains,
        cut,
        scratch=[pltpu.VMEM((24, LANES), F32), pltpu.VMEM(share, F32)],
        name="last",
    )
    mixed = exchanged(mixed, ("freq", "c"))
    members = times // CHANS
    copies = call(functools.partial(joined_kernel, fit_weights(count)), (members, 64, LANES), mixed, name="joined")
    everything = exchanged(copies, ("r1", "g", "r0"))
    other = lax.ppermute(everything[:, 32:], "freq", [(i, i ^ 1) for i in range(freqs)])
    block = (CHANS, 8, DIRS, STATIONS)
    held = [pltpu.VMEM(block, F32), pltpu.VMEM(block, F32), pltpu.SemaphoreType.DMA((2,))]
    full = (POLY, 8, DIRS, STATIONS)
    everything = in_vmem(everything.reshape(members * 64, LANES))
    gains, half, part = pl.pallas_call(
        functools.partial(near_kernel, count),
        out_shape=(pltpu.HBM(block, F32), pltpu.HBM(full, F32), pltpu.VMEM(block, F32)),
        in_specs=[VMEM, VMEM],
        out_specs=(HBM, HBM, VMEM),
        scratch_shapes=held,
        compiler_params=pltpu.CompilerParams(vmem_limit_bytes=12 << 20),
        cost_estimate=pl.CostEstimate(flops=1000000, bytes_accessed=2000000, transcendentals=0),
        name="near",
    )(everything, in_vmem(duals_start))
    duals, polynomial = pl.pallas_call(
        functools.partial(far_kernel, count),
        out_shape=(pltpu.HBM(block, F32), pltpu.HBM(full, F32)),
        in_specs=[VMEM, VMEM, HBM],
        out_specs=(HBM, HBM),
        input_output_aliases={2: 1},
        scratch_shapes=held,
        compiler_params=pltpu.CompilerParams(vmem_limit_bytes=12 << 20),
        name="far",
    )(in_vmem(other.reshape(members * 32, LANES)), part, half)
    return (gains, duals, polynomial)


def solution(mesh):
    freqs = mesh.shape["freq"]
    fine = Mesh(mesh.devices.reshape(freqs, CHANS, 2, GROUPS, 2), ("freq", *TIMES))
    placed = (
        P("freq", None, TIMES),
        P("freq", None, None, TIMES),
        P(None, TIMES),
        P("freq", None, None, None),
        P("freq", None, None, None),
        P(),
    )
    return jax.shard_map(
        shards,
        mesh=fine,
        in_specs=placed,
        out_specs=(P("freq", None, None, None), P("freq", None, None, None), P()),
        check_vma=False,
    )
```

```python
import functools

import jax
import jax.numpy as jnp
import numpy as np
from jax import lax
from jax.experimental import pallas as pl
from jax.experimental.pallas import tpu as pltpu
from jax.sharding import Mesh
from jax.sharding import PartitionSpec as P

ITERS = 2
RHO = 16.0
CHANS = 2
DIRS = 8
STATIONS = 512
ROWS = 128
POLY = 4
LANES = 128
CUTS = STATIONS // LANES
GROUPS = 4
PAIR = DIRS // GROUPS
SOURCES = CHANS * GROUPS
HALF = 4
F32 = jnp.float32
BF16 = jnp.bfloat16


def adjoint(matrix):
    re, im = matrix
    return ([re[0], re[2], re[1], re[3]], [-im[0], -im[2], -im[1], -im[3]])


def product(left, right):
    lr, li = left
    rr, ri = right
    out_re, out_im = [], []
    for row in range(2):
        for col in range(2):
            a = 2 * row
            out_re.append(lr[a] * rr[col] - li[a] * ri[col] + lr[a + 1] * rr[col + 2] - li[a + 1] * ri[col + 2])
            out_im.append(lr[a] * ri[col] + li[a] * rr[col] + lr[a + 1] * ri[col + 2] + li[a + 1] * rr[col + 2])
    return (out_re, out_im)


def normal(matrix):
    re, im = matrix
    return [
        re[0] ** 2 + im[0] ** 2 + re[1] ** 2 + im[1] ** 2,
        re[2] ** 2 + im[2] ** 2 + re[3] ** 2 + im[3] ** 2,
        re[0] * re[2] + im[0] * im[2] + re[1] * re[3] + im[1] * im[3],
        im[0] * re[2] - re[0] * im[2] + im[1] * re[3] - re[1] * im[3],
    ]


def two_parts(x):
    high = x.astype(BF16)
    low = (x - high.astype(F32)).astype(BF16)
    return jnp.concatenate([high, low], axis=0)


VMEM = pl.BlockSpec(memory_space=pltpu.VMEM)
HBM = pl.BlockSpec(memory_space=pltpu.HBM)


def in_vmem(x):
    return pltpu.with_memory_space_constraint(x, pltpu.MemorySpace.VMEM)


def call(kernel, outs, *args, scratch=(), fast=None, kinds=None, limit=12 << 20, name=None):
    fast = range(len(args)) if fast is None else fast
    args = [in_vmem(a) if n in fast else a for n, a in enumerate(args)]
    many = isinstance(outs, list)
    kinds = kinds or [F32] * len(outs)
    return pl.pallas_call(
        kernel,
        out_shape=tuple(pltpu.VMEM(o, t) for o, t in zip(outs, kinds)) if many else pltpu.VMEM(outs, F32),
        in_specs=[VMEM for _ in args],
        out_specs=tuple(VMEM for _ in outs) if many else VMEM,
        scratch_shapes=list(scratch),
        compiler_params=pltpu.CompilerParams(vmem_limit_bytes=limit),
        name=name,
    )(*args)


def basis_of(channel, count):
    x = (2.0 * channel.astype(F32) + 1.0) / count - 1.0
    return [1.0 + 0.0 * x, x, 1.5 * x * x - 0.5, 2.5 * x * x * x - 1.5 * x]


def fit_weights(count):
    x = (2.0 * np.arange(count) + 1.0) / count - 1.0
    basis = np.stack([np.ones_like(x), x, 1.5 * x * x - 0.5, 2.5 * x**3 - 1.5 * x], axis=1)
    return np.linalg.solve(basis.T @ basis, basis.T)


def split(parts):
    return (parts[:4], parts[4:])


def flat(matrix):
    return matrix[0] + matrix[1]


def pack_kernel(gains_ref, coh_ref, vis_ref, pairs_ref, out_ref, sky):
    station = lax.broadcasted_iota(jnp.int32, (STATIONS, ROWS), 0)
    hot = [jnp.where(station == pairs_ref[i : i + 1, :], 1.0, 0.0) for i in range(2)]
    hot = jnp.concatenate(hot, axis=1).astype(BF16)
    rows = gains_ref[...].reshape(CHANS * 8 * DIRS, STATIONS)
    found = jnp.dot(two_parts(rows), hot, preferred_element_type=F32)
    found = found[: rows.shape[0]] + found[rows.shape[0] :]
    names = jnp.concatenate(
        [pairs_ref[0:2, :].astype(F32), jnp.zeros((6, ROWS), F32)],
        axis=0,
    )
    for c in range(CHANS):
        at = [found[(c * 8 + i) * DIRS : (c * 8 + i + 1) * DIRS] for i in range(8)]
        first = split([a[:, :ROWS] for a in at])
        second = split([a[:, ROWS:] for a in at])
        parts = [coh_ref[c, i].astype(F32) for i in range(8)]
        for i in range(8):
            sky[c, pl.ds(i * DIRS, DIRS), :] = parts[i]
        model = flat(product(product(first, split(parts)), adjoint(second)))
        rest = vis_ref[c] - jnp.concatenate([jnp.sum(m, axis=0, keepdims=True) for m in model], axis=0)
        for g in range(GROUPS):
            for d in range(PAIR):
                out_ref[c * GROUPS + g, pl.ds(d * 8, 8), :] = sky[c, pl.ds(d * GROUPS + g, 8, stride=DIRS), :]
            out_ref[c * GROUPS + g, pl.ds(16, 8), :] = rest
            out_ref[c * GROUPS + g, pl.ds(24, 8), :] = names


def place_of():
    own = lax.axis_index("r1") * 2 + lax.axis_index("r0")
    return lax.axis_index("freq"), lax.axis_index("c"), lax.axis_index("g"), own


def own_kernel(count, gains_ref, duals_ref, poly_ref, out_ref, cut_ref):
    freq, c, g, own = place_of()
    basis = basis_of(freq * CHANS + c, count)
    sublane = lax.broadcasted_iota(jnp.int32, (DIRS, STATIONS), 0)
    for i in range(8):
        prior = basis[0] * poly_ref[0, i]
        for j in range(1, POLY):
            prior += basis[j] * poly_ref[j, i]
        for n, tile in enumerate((gains_ref[c, i], duals_ref[c, i], prior)):
            for d in range(PAIR):
                row = jnp.sum(jnp.where(sublane == d * GROUPS + g, tile, 0.0), axis=0, keepdims=True)
                parts = [row[:, q * LANES : (q + 1) * LANES] for q in range(CUTS)]
                chosen = parts[0]
                for q in range(CUTS):
                    out_ref[n, pl.ds(i * 8 + q * PAIR + d, 1), :] = parts[q]
                    chosen = jnp.where(own == q, parts[q], chosen)
                cut_ref[n, pl.ds(d * 8 + i, 1), :] = chosen


def looked_up(gains_ref, hot_ref, at_ref):
    rows = jnp.concatenate(
        [
            jnp.concatenate(
                [gains_ref[pl.ds(q * PAIR + d, 8, stride=8), :] for q in range(CUTS)], axis=1
            )
            for d in range(PAIR)
        ],
        axis=0,
    )
    found = jnp.dot(two_parts(rows), hot_ref[...], preferred_element_type=F32)
    found = found[:16] + found[16:]
    for b in range(2 * SOURCES):
        at_ref[pl.ds(b * 16, 16), :] = found[:, b * ROWS : (b + 1) * ROWS]


def ends(at_ref, d):
    first = [at_ref[pl.ds(d * 8 + i, SOURCES, stride=16), :] for i in range(8)]
    second = [at_ref[pl.ds(SOURCES * 16 + d * 8 + i, SOURCES, stride=16), :] for i in range(8)]
    return split(first), split(second)


def sky_of(rows_ref, d):
    return split([rows_ref[pl.ds(d * 8 + i, SOURCES, stride=32), :] for i in range(8)])


def summed(rest, rows_ref, at_ref, hot_ref, terms, total_ref):
    half = SOURCES * 24
    for d in range(PAIR):
        first, second = ends(at_ref, d)
        sky = sky_of(rows_ref, d)
        left = product(first, sky)
        right = product(sky, adjoint(second))
        ahead = flat(product(rest, adjoint(right))) + normal(right)
        behind = flat(product(adjoint(rest), left)) + normal(adjoint(left))
        for i in range(12):
            terms[pl.ds(d * 12 + i, SOURCES, stride=24), :] = ahead[i]
            terms[pl.ds(half + d * 12 + i, SOURCES, stride=24), :] = behind[i]
    wide = jnp.concatenate([terms[pl.ds(b * 24, 24), :] for b in range(2 * SOURCES)], axis=1)
    total = lax.dot_general(
        two_parts(wide), hot_ref[...], (((1,), (1,)), ((), ())), preferred_element_type=F32
    )
    total = total[:24] + total[24:]
    for q in range(CUTS):
        total_ref[q] = total[:, q * LANES : (q + 1) * LANES]


def model_of(rows_ref, at_ref):
    model = None
    for d in range(PAIR):
        first, second = ends(at_ref, d)
        part = flat(product(product(first, sky_of(rows_ref, d)), adjoint(second)))
        model = part if model is None else [a + b for a, b in zip(model, part)]
    return model


def start_kernel(rows_ref, own_ref, out_ref, hot_ref, model_ref, at, terms, total):
    station = lax.broadcasted_iota(jnp.int32, (STATIONS, ROWS), 0).astype(F32)
    for end in range(2):
        for n in range(SOURCES):
            name = rows_ref[pl.ds(n * 32 + 24 + end, 1), :]
            lanes = pl.ds((end * SOURCES + n) * ROWS, ROWS)
            hot_ref[:, lanes] = jnp.where(station == name, 1.0, 0.0).astype(BF16)
    looked_up(own_ref.at[0], hot_ref, at)
    rest = split([rows_ref[pl.ds(16 + i, SOURCES, stride=32), :] for i in range(8)])
    summed(rest, rows_ref, at, hot_ref, terms, total)
    for q in range(CUTS):
        for d in range(PAIR):
            part = total[q, pl.ds(d * 12, 12), :]
            for n in range(out_ref.shape[0]):
                out_ref[n, pl.ds(q * PAIR + d, 12, stride=8), :] = part
    model = model_of(rows_ref, at)
    for i in range(8):
        model_ref[pl.ds(i * 8, 8), :] = model[i]


def stepped(total, gains, duals, prior, damping):
    way = [total[i] - duals[i] - RHO * (gains[i] - prior[i]) for i in range(8)]
    top, bottom, cross_re, cross_im = total[8:]
    shift = damping * 0.5 * (top + bottom) + RHO
    upper = top + shift
    lower = bottom + shift
    scale = 1.0 / (upper * lower - cross_re * cross_re - cross_im * cross_im)
    zeros = jnp.zeros_like(scale)
    inverse = (
        [lower * scale, -cross_re * scale, -cross_re * scale, upper * scale],
        [zeros, -cross_im * scale, cross_im * scale, zeros],
    )
    step = flat(product(split(way), inverse))
    return [gains[i] + step[i] for i in range(8)]


def middle_kernel(
    damping, arrived, own_ref, rows_ref, hot_ref, model_ref, out_ref, cut_ref, at_ref, gains_ref
):
    own = place_of()[3]
    total = []
    for i in range(12):
        value = arrived[0, pl.ds(i * 8, 8), :]
        for n in range(1, arrived.shape[0]):
            value = value + arrived[n, pl.ds(i * 8, 8), :]
        total.append(value)
    start = [[own_ref[n, pl.ds(i * 8, 8), :] for i in range(8)] for n in range(3)]
    new = stepped(total, *start, damping)
    for i in range(8):
        gains_ref[pl.ds(i * 8, 8), :] = new[i]
        chosen = new[i][:PAIR]
        for q in range(1, CUTS):
            chosen = jnp.where(own == q, new[i][q * PAIR : (q + 1) * PAIR], chosen)
        cut_ref[pl.ds(i, PAIR, stride=8), :] = chosen
    looked_up(gains_ref, hot_ref, at_ref)
    model = model_of(rows_ref, at_ref)
    for i in range(8):
        change = model_ref[pl.ds(i * 8, 8), :] - model[i]
        for n in range(out_ref.shape[0]):
            out_ref[n, pl.ds(i * 8, 8), :] = change


def second_kernel(arrived, rows_ref, hot_ref, at_ref, out_ref, terms):
    rest = []
    for i in range(8):
        value = rows_ref[pl.ds(16 + i, SOURCES, stride=32), :]
        for n in range(arrived.shape[0]):
            value = value + arrived[n, pl.ds(i * 8, 8), :]
        rest.append(value)
    summed(split(rest), rows_ref, at_ref, hot_ref, terms, out_ref)


def last_kernel(damping, arrived, gains_ref, own_ref, out_ref, total_ref, mixed_ref):
    value = arrived[0]
    for n in range(1, arrived.shape[0]):
        value = value + arrived[n]
    total_ref[...] = value
    total = [total_ref[pl.ds(i, PAIR, stride=12), :] for i in range(12)]
    gains = [gains_ref[pl.ds(i, PAIR, stride=8), :] for i in range(8)]
    duals, prior = [[own_ref[n, pl.ds(i, PAIR, stride=8), :] for i in range(8)] for n in (1, 2)]
    new = stepped(total, gains, duals, prior, damping)
    for i in range(8):
        mixed_ref[i // HALF, pl.ds(i % HALF, PAIR, stride=HALF), :] = new[i] + duals[i] / RHO
    for n in range(out_ref.shape[0]):
        out_ref[n] = mixed_ref[n // CHANS % 2]


def joined_kernel(weights, arrived, out_ref):
    freq = lax.axis_index("freq")
    twin = freq + 1 - 2 * (freq % 2)
    parts = [arrived[f * CHANS + c] for f in (freq, twin) for c in range(CHANS)]
    mixed = [arrived[n] for n in range(arrived.shape[0])]
    for j in range(POLY):
        total = float(weights[j, 0]) * mixed[0]
        for n in range(1, len(mixed)):
            total = total + float(weights[j, n]) * mixed[n]
        parts.append(total)
    for n in range(out_ref.shape[0]):
        for k, part in enumerate(parts):
            out_ref[n, pl.ds(k * 8, 8), :] = part


def tile_of(ref, q, row, size):
    place = (q // 2) * 8 + q % 2
    return jnp.concatenate(
        [ref[pl.ds(place * size + row + d * HALF, GROUPS, stride=2 * size), :] for d in range(PAIR)], axis=0
    )


def put_half(count, far, ref, size, poly_at, duals_ref, outs, held, sems):
    freq = lax.axis_index("freq")
    side = 1 - freq % 2 if far else freq % 2
    basis = [basis_of(freq * CHANS + c, count) for c in range(CHANS)]
    gains, duals, poly = held
    to_gains, to_duals, to_poly = [
        pltpu.make_async_copy(a, b.at[:, pl.ds(HALF * side, HALF)], sems.at[n])
        for n, (a, b) in enumerate(zip(held, outs))
    ]
    for i in range(HALF):
        for j in range(POLY):
            for q in range(CUTS):
                poly[j, i, :, q * LANES : (q + 1) * LANES] = tile_of(ref, q, poly_at + j * 8 + i, size)
    to_poly.start()
    for c in range(CHANS):
        for i in range(HALF):
            mixed = jnp.concatenate([tile_of(ref, q, c * 8 + i, size) for q in range(CUTS)], axis=1)
            gains[c, i] = mixed - duals_ref[c, HALF * side + i] / RHO
            duals[c, i] = RHO * (mixed - sum(basis[c][j] * poly[j, i] for j in range(POLY)))
    to_gains.start()
    to_duals.start()
    to_poly.wait()
    to_gains.wait()
    to_duals.wait()


def near_kernel(count, ref, duals_ref, gains_out, duals_out, poly_out, gains, duals, poly, sems):
    outs = (gains_out, duals_out, poly_out)
    put_half(count, False, ref, 64, 32, duals_ref, outs, (gains, duals, poly), sems)


def far_kernel(count, ref, duals_ref, _g, _d, _p, gains_out, duals_out, poly_out, gains, duals, poly, sems):
    outs = (gains_out, duals_out, poly_out)
    put_half(count, True, ref, 48, 16, duals_ref, outs, (gains, duals, poly), sems)


def exchanged(x, axis):
    return lax.all_to_all(x, axis, split_axis=0, concat_axis=0, tiled=True)


TIMES = ("c", "r1", "g", "r0")


def shards(visibilities, coherencies, pairs, gains_start, duals_start, poly_start):
    freqs = lax.axis_size("freq")
    times = lax.axis_size(TIMES)
    count = CHANS * freqs
    sums_shape = (CUTS, 12 * 8, LANES)
    tiles = (64, LANES)
    share = (16, LANES)
    work = pltpu.VMEM((2 * SOURCES * 24, ROWS), F32)
    quarters = (CUTS, 24, LANES)

    sent = call(
        pack_kernel,
        (SOURCES, 32, ROWS),
        gains_start,
        coherencies,
        visibilities,
        pairs,
        fast=[],
        limit=60 << 20,
        scratch=[pltpu.VMEM((CHANS, 64, ROWS), F32)],
        name="pack",
    )
    own, cut = call(
        functools.partial(own_kernel, count),
        [(3, *tiles), (3, *share)],
        gains_start,
        duals_start,
        poly_start,
        fast=[],
        limit=60 << 20,
        name="own",
    )
    rows = exchanged(sent, ("c", "g")).reshape(SOURCES * 32, ROWS)
    sums, hot, model = call(
        start_kernel,
        [sums_shape, (STATIONS, 2 * SOURCES * ROWS), tiles],
        rows,
        own,
        kinds=[F32, BF16, F32],
        scratch=[pltpu.VMEM((2 * SOURCES * 16, ROWS), F32), work, pltpu.VMEM(quarters, F32)],
        name="start",
    )
    sums = exchanged(sums, ("r1", "r0"))
    change, gains, at = call(
        functools.partial(middle_kernel, 12.0),
        [(GROUPS, *tiles), share, (2 * SOURCES * 16, ROWS)],
        sums,
        own,
        rows,
        hot,
        model,
        scratch=[pltpu.VMEM(tiles, F32)],
        name="middle",
    )
    change = exchanged(change, "g")
    sums = call(second_kernel, quarters, change, rows, hot, at, scratch=[work], name="second")
    sums = exchanged(sums, ("r1", "r0"))
    mixed = call(
        functools.partial(last_kernel, 6.0),
        (freqs * CHANS, 8, LANES),
        sums,
        gains,
        cut,
        scratch=[pltpu.VMEM((24, LANES), F32), pltpu.VMEM((2, 8, LANES), F32)],
        name="last",
    )
    mixed = exchanged(mixed, ("freq", "c"))
    members = times // CHANS
    copies = call(functools.partial(joined_kernel, fit_weights(count)), (members, 64, LANES), mixed, name="joined")
    everything = exchanged(copies, ("r1", "g", "r0"))
    other = lax.ppermute(everything[:, 16:], "freq", [(i, i ^ 1) for i in range(freqs)])
    block = (CHANS, 8, DIRS, STATIONS)
    outs = (pltpu.HBM(block, F32), pltpu.HBM(block, F32), pltpu.HBM((POLY, 8, DIRS, STATIONS), F32))
    held = [pltpu.VMEM((n, HALF, DIRS, STATIONS), F32) for n in (CHANS, CHANS, POLY)]
    options = dict(
        out_shape=outs,
        out_specs=(HBM, HBM, HBM),
        scratch_shapes=[*held, pltpu.SemaphoreType.DMA((3,))],
        compiler_params=pltpu.CompilerParams(vmem_limit_bytes=12 << 20),
    )
    duals_start = in_vmem(duals_start)
    halves = pl.pallas_call(
        functools.partial(near_kernel, count),
        in_specs=[VMEM, VMEM],
        cost_estimate=pl.CostEstimate(flops=1000000, bytes_accessed=2000000, transcendentals=0),
        name="near",
        **options,
    )(in_vmem(everything.reshape(members * 64, LANES)), duals_start)
    return pl.pallas_call(
        functools.partial(far_kernel, count),
        in_specs=[VMEM, VMEM, HBM, HBM, HBM],
        input_output_aliases={2: 0, 3: 1, 4: 2},
        name="far",
        **options,
    )(in_vmem(other.reshape(members * 48, LANES)), duals_start, *halves)


def solution(mesh):
    freqs = mesh.shape["freq"]
    fine = Mesh(mesh.devices.reshape(freqs, CHANS, 2, GROUPS, 2), ("freq", *TIMES))
    placed = (
        P("freq", None, TIMES),
        P("freq", None, None, TIMES),
        P(None, TIMES),
        P("freq", None, None, None),
        P("freq", None, None, None),
        P(),
    )
    return jax.shard_map(
        shards,
        mesh=fine,
        in_specs=placed,
        out_specs=(P("freq", None, None, None), P("freq", None, None, None), P()),
        check_vma=False,
    )
```

```python
import functools

import jax
import jax.numpy as jnp
import numpy as np
from jax import lax
from jax.experimental import pallas as pl
from jax.experimental.pallas import tpu as pltpu
from jax.sharding import Mesh
from jax.sharding import PartitionSpec as P

ITERS = 2
RHO = 16.0
CHANS = 2
DIRS = 8
STATIONS = 512
ROWS = 128
POLY = 4
LANES = 128
CUTS = STATIONS // LANES
GROUPS = 4
PAIR = DIRS // GROUPS
SOURCES = CHANS * GROUPS
HALF = 4
F32 = jnp.float32
BF16 = jnp.bfloat16


def adjoint(matrix):
    re, im = matrix
    return ([re[0], re[2], re[1], re[3]], [-im[0], -im[2], -im[1], -im[3]])


def product(left, right):
    lr, li = left
    rr, ri = right
    out_re, out_im = [], []
    for row in range(2):
        for col in range(2):
            a = 2 * row
            out_re.append(lr[a] * rr[col] - li[a] * ri[col] + lr[a + 1] * rr[col + 2] - li[a + 1] * ri[col + 2])
            out_im.append(lr[a] * ri[col] + li[a] * rr[col] + lr[a + 1] * ri[col + 2] + li[a + 1] * rr[col + 2])
    return (out_re, out_im)


def normal(matrix):
    re, im = matrix
    return [
        re[0] ** 2 + im[0] ** 2 + re[1] ** 2 + im[1] ** 2,
        re[2] ** 2 + im[2] ** 2 + re[3] ** 2 + im[3] ** 2,
        re[0] * re[2] + im[0] * im[2] + re[1] * re[3] + im[1] * im[3],
        im[0] * re[2] - re[0] * im[2] + im[1] * re[3] - re[1] * im[3],
    ]


def two_parts(x):
    high = x.astype(BF16)
    low = (x - high.astype(F32)).astype(BF16)
    return jnp.concatenate([high, low], axis=0)


VMEM = pl.BlockSpec(memory_space=pltpu.VMEM)
HBM = pl.BlockSpec(memory_space=pltpu.HBM)


def in_hbm(x):
    return pltpu.with_memory_space_constraint(x, pltpu.MemorySpace.HBM)


def in_vmem(x):
    return pltpu.with_memory_space_constraint(x, pltpu.MemorySpace.VMEM)


def call(kernel, outs, *args, scratch=(), fast=None, kinds=None, far=(), limit=12 << 20, name=None):
    fast = range(len(args)) if fast is None else fast
    args = [in_vmem(a) if n in fast else in_hbm(a) if n in far else a for n, a in enumerate(args)]
    many = isinstance(outs, list)
    kinds = kinds or [F32] * len(outs)
    return pl.pallas_call(
        kernel,
        out_shape=tuple(pltpu.VMEM(o, t) for o, t in zip(outs, kinds)) if many else pltpu.VMEM(outs, F32),
        in_specs=[HBM if n in far else VMEM for n in range(len(args))],
        out_specs=tuple(VMEM for _ in outs) if many else VMEM,
        scratch_shapes=list(scratch),
        compiler_params=pltpu.CompilerParams(vmem_limit_bytes=limit),
        name=name,
    )(*args)


def basis_of(channel, count):
    x = (2.0 * channel.astype(F32) + 1.0) / count - 1.0
    return [1.0 + 0.0 * x, x, 1.5 * x * x - 0.5, 2.5 * x * x * x - 1.5 * x]


def fit_weights(count):
    x = (2.0 * np.arange(count) + 1.0) / count - 1.0
    basis = np.stack([np.ones_like(x), x, 1.5 * x * x - 0.5, 2.5 * x**3 - 1.5 * x], axis=1)
    return np.linalg.solve(basis.T @ basis, basis.T)


def split(parts):
    return (parts[:4], parts[4:])


def flat(matrix):
    return matrix[0] + matrix[1]


def pack_kernel(gains_ref, coh_ref, vis_ref, pairs_ref, out_ref, own_ref, sky):
    station = lax.broadcasted_iota(jnp.int32, (STATIONS, ROWS), 0)
    hot = [jnp.where(station == pairs_ref[i : i + 1, :], 1.0, 0.0) for i in range(2)]
    hot = jnp.concatenate(hot, axis=1).astype(BF16)
    rows = gains_ref[...].reshape(CHANS * 8 * DIRS, STATIONS)
    found = jnp.dot(two_parts(rows), hot, preferred_element_type=F32)
    found = found[: rows.shape[0]] + found[rows.shape[0] :]
    names = jnp.concatenate(
        [pairs_ref[0:2, :].astype(F32), jnp.zeros((6, ROWS), F32)],
        axis=0,
    )
    for c in range(CHANS):
        at = [found[(c * 8 + i) * DIRS : (c * 8 + i + 1) * DIRS] for i in range(8)]
        first = split([a[:, :ROWS] for a in at])
        second = split([a[:, ROWS:] for a in at])
        parts = [coh_ref[c, i].astype(F32) for i in range(8)]
        for i in range(8):
            sky[c, pl.ds(i * DIRS, DIRS), :] = parts[i]
        model = flat(product(product(first, split(parts)), adjoint(second)))
        rest = vis_ref[c] - jnp.concatenate([jnp.sum(m, axis=0, keepdims=True) for m in model], axis=0)
        for g in range(GROUPS):
            for d in range(PAIR):
                out_ref[c * GROUPS + g, pl.ds(d * 8, 8), :] = sky[c, pl.ds(d * GROUPS + g, 8, stride=DIRS), :]
            out_ref[c * GROUPS + g, pl.ds(16, 8), :] = rest
            out_ref[c * GROUPS + g, pl.ds(24, 8), :] = names
    _, c, g, _ = place_of()
    for i in range(8):
        to_rows(gains_ref[c, i], i, g, own_ref)


def place_of():
    own = lax.axis_index("r1") * 2 + lax.axis_index("r0")
    return lax.axis_index("freq"), lax.axis_index("c"), lax.axis_index("g"), own


def to_rows(tile, i, g, put):
    sublane = lax.broadcasted_iota(jnp.int32, (DIRS, STATIONS), 0)
    for d in range(PAIR):
        row = jnp.sum(jnp.where(sublane == d * GROUPS + g, tile, 0.0), axis=0, keepdims=True)
        for q in range(CUTS):
            put[pl.ds(i * 8 + q * PAIR + d, 1), :] = row[:, q * LANES : (q + 1) * LANES]


def by_component(gains_ref):
    rows = jnp.concatenate(
        [
            jnp.concatenate(
                [gains_ref[pl.ds(q * PAIR + d, 8, stride=8), :] for q in range(CUTS)], axis=1
            )
            for d in range(PAIR)
        ],
        axis=0,
    )
    return two_parts(rows)


def look_up(parts, hot, at_ref, block):
    found = jnp.dot(parts, hot, preferred_element_type=F32)
    found = found[:16] + found[16:]
    for b in range(hot.shape[1] // ROWS):
        at_ref[pl.ds((block + b) * 16, 16), :] = found[:, b * ROWS : (b + 1) * ROWS]


def ends(at_ref, d):
    first = [at_ref[pl.ds(d * 8 + i, SOURCES, stride=16), :] for i in range(8)]
    second = [at_ref[pl.ds(SOURCES * 16 + d * 8 + i, SOURCES, stride=16), :] for i in range(8)]
    return split(first), split(second)


def sky_of(rows_ref, d):
    return split([rows_ref[pl.ds(d * 8 + i, SOURCES, stride=32), :] for i in range(8)])


def summed(rest, rows_ref, at_ref, hot_ref, terms, total_ref):
    half = SOURCES * 24
    for d in range(PAIR):
        first, second = ends(at_ref, d)
        sky = sky_of(rows_ref, d)
        left = product(first, sky)
        right = product(sky, adjoint(second))
        ahead = flat(product(rest, adjoint(right))) + normal(right)
        behind = flat(product(adjoint(rest), left)) + normal(adjoint(left))
        for i in range(12):
            terms[pl.ds(d * 12 + i, SOURCES, stride=24), :] = ahead[i]
            terms[pl.ds(half + d * 12 + i, SOURCES, stride=24), :] = behind[i]
    wide = jnp.concatenate([terms[pl.ds(b * 24, 24), :] for b in range(2 * SOURCES)], axis=1)
    total = lax.dot_general(
        two_parts(wide), hot_ref[...], (((1,), (1,)), ((), ())), preferred_element_type=F32
    )
    total = total[:24] + total[24:]
    for q in range(CUTS):
        total_ref[q] = total[:, q * LANES : (q + 1) * LANES]


def model_of(rows_ref, at_ref):
    model = None
    for d in range(PAIR):
        first, second = ends(at_ref, d)
        part = flat(product(product(first, sky_of(rows_ref, d)), adjoint(second)))
        model = part if model is None else [a + b for a, b in zip(model, part)]
    return model


def start_kernel(
    rows_ref,
    own_ref,
    duals_far,
    poly_far,
    out_ref,
    hot_ref,
    model_ref,
    duals_ref,
    poly_ref,
    at,
    terms,
    total,
    sems,
):
    loads = [
        pltpu.make_async_copy(duals_far, duals_ref, sems.at[0]),
        pltpu.make_async_copy(poly_far, poly_ref, sems.at[1]),
    ]
    for load in loads:
        load.start()
    shape = (STATIONS // 16, 16, ROWS)
    station = lax.broadcasted_iota(jnp.int32, (STATIONS, ROWS), 0).astype(jnp.int16).reshape(shape)

    def marked(name):
        wide = jnp.broadcast_to(name.astype(jnp.int32), (16, ROWS)).astype(jnp.int16)
        mark = jnp.where(station == wide[None], jnp.ones((), BF16), jnp.zeros((), BF16))
        return mark.reshape(STATIONS, ROWS)

    parts = by_component(own_ref)
    for b in range(0, 2 * SOURCES, 2):
        hot = []
        for n in (b, b + 1):
            end, source = n // SOURCES, n % SOURCES
            hot.append(marked(rows_ref[pl.ds(source * 32 + 24 + end, 1), :]))
        hot = jnp.concatenate(hot, axis=1)
        hot_ref[:, b * ROWS : (b + 2) * ROWS] = hot
        look_up(parts, hot, at, b)
    rest = split([rows_ref[pl.ds(16 + i, SOURCES, stride=32), :] for i in range(8)])
    summed(rest, rows_ref, at, hot_ref, terms, total)
    for q in range(CUTS):
        for d in range(PAIR):
            part = total[q, pl.ds(d * 12, 12), :]
            for n in range(out_ref.shape[0]):
                out_ref[n, pl.ds(q * PAIR + d, 12, stride=8), :] = part
    model = model_of(rows_ref, at)
    for i in range(8):
        model_ref[pl.ds(i * 8, 8), :] = model[i]
    for load in loads:
        load.wait()


def stepped(total, gains, duals, prior, damping):
    way = [total[i] - duals[i] - RHO * (gains[i] - prior[i]) for i in range(8)]
    top, bottom, cross_re, cross_im = total[8:]
    shift = damping * 0.5 * (top + bottom) + RHO
    upper = top + shift
    lower = bottom + shift
    scale = 1.0 / (upper * lower - cross_re * cross_re - cross_im * cross_im)
    zeros = jnp.zeros_like(scale)
    inverse = (
        [lower * scale, -cross_re * scale, -cross_re * scale, upper * scale],
        [zeros, -cross_im * scale, cross_im * scale, zeros],
    )
    step = flat(product(split(way), inverse))
    return [gains[i] + step[i] for i in range(8)]


def middle_kernel(
    damping,
    count,
    arrived,
    own_ref,
    duals_ref,
    poly_ref,
    rows_ref,
    hot_ref,
    model_ref,
    out_ref,
    cut_ref,
    at_ref,
    gains_ref,
    other_ref,
):
    freq, c, g, own = place_of()
    basis = basis_of(freq * CHANS + c, count)
    for i in range(8):
        to_rows(duals_ref[c, i], i, g, other_ref.at[0])
        to_rows(sum(basis[j] * poly_ref[j, i] for j in range(POLY)), i, g, other_ref.at[1])
    total = []
    for i in range(12):
        value = arrived[0, pl.ds(i * 8, 8), :]
        for n in range(1, arrived.shape[0]):
            value = value + arrived[n, pl.ds(i * 8, 8), :]
        total.append(value)
    start = [[ref[pl.ds(i * 8, 8), :] for i in range(8)] for ref in (own_ref, other_ref.at[0], other_ref.at[1])]
    new = stepped(total, *start, damping)
    for i in range(8):
        gains_ref[pl.ds(i * 8, 8), :] = new[i]
        for n, tile in enumerate((new[i], start[1][i], start[2][i])):
            chosen = tile[:PAIR]
            for q in range(1, CUTS):
                chosen = jnp.where(own == q, tile[q * PAIR : (q + 1) * PAIR], chosen)
            cut_ref[n, pl.ds(i, PAIR, stride=8), :] = chosen
    look_up(by_component(gains_ref), hot_ref[...], at_ref, 0)
    model = model_of(rows_ref, at_ref)
    for i in range(8):
        change = model_ref[pl.ds(i * 8, 8), :] - model[i]
        for n in range(out_ref.shape[0]):
            out_ref[n, pl.ds(i * 8, 8), :] = change


def second_kernel(arrived, rows_ref, hot_ref, at_ref, out_ref, terms):
    rest = []
    for i in range(8):
        value = rows_ref[pl.ds(16 + i, SOURCES, stride=32), :]
        for n in range(arrived.shape[0]):
            value = value + arrived[n, pl.ds(i * 8, 8), :]
        rest.append(value)
    summed(split(rest), rows_ref, at_ref, hot_ref, terms, out_ref)


def last_kernel(damping, arrived, own_ref, out_ref, total_ref, mixed_ref):
    value = arrived[0]
    for n in range(1, arrived.shape[0]):
        value = value + arrived[n]
    total_ref[...] = value
    total = [total_ref[pl.ds(i, PAIR, stride=12), :] for i in range(12)]
    gains, duals, prior = [[own_ref[n, pl.ds(i, PAIR, stride=8), :] for i in range(8)] for n in range(3)]
    new = stepped(total, gains, duals, prior, damping)
    for i in range(8):
        mixed_ref[i // HALF, pl.ds(i % HALF, PAIR, stride=HALF), :] = new[i] + duals[i] / RHO
    for n in range(out_ref.shape[0]):
        out_ref[n] = mixed_ref[n // CHANS % 2]


def joined_kernel(weights, arrived, out_ref):
    freq = lax.axis_index("freq")
    twin = freq + 1 - 2 * (freq % 2)
    parts = [arrived[f * CHANS + c] for f in (freq, twin) for c in range(CHANS)]
    mixed = [arrived[n] for n in range(arrived.shape[0])]
    for j in range(POLY):
        total = float(weights[j, 0]) * mixed[0]
        for n in range(1, len(mixed)):
            total = total + float(weights[j, n]) * mixed[n]
        parts.append(total)
    for n in range(out_ref.shape[0]):
        for k, part in enumerate(parts):
            out_ref[n, pl.ds(k * 8, 8), :] = part


def tile_of(ref, q, row, size):
    place = (q // 2) * 8 + q % 2
    return jnp.concatenate(
        [ref[pl.ds(place * size + row + d * HALF, GROUPS, stride=2 * size), :] for d in range(PAIR)], axis=0
    )


def put_half(count, far, ref, size, poly_at, duals_ref, outs, held, sems):
    freq = lax.axis_index("freq")
    side = 1 - freq % 2 if far else freq % 2
    basis = [basis_of(freq * CHANS + c, count) for c in range(CHANS)]
    gains, duals, poly = held
    to_gains, to_duals, to_poly = [
        pltpu.make_async_copy(a, b.at[:, pl.ds(HALF * side, HALF)], sems.at[n])
        for n, (a, b) in enumerate(zip(held, outs))
    ]
    for i in range(HALF):
        for j in range(POLY):
            for q in range(CUTS):
                poly[j, i, :, q * LANES : (q + 1) * LANES] = tile_of(ref, q, poly_at + j * 8 + i, size)
    to_poly.start()
    for c in range(CHANS):
        for i in range(HALF):
            mixed = jnp.concatenate([tile_of(ref, q, c * 8 + i, size) for q in range(CUTS)], axis=1)
            gains[c, i] = mixed - duals_ref[c, HALF * side + i] / RHO
            duals[c, i] = RHO * (mixed - sum(basis[c][j] * poly[j, i] for j in range(POLY)))
    to_gains.start()
    to_duals.start()
    to_poly.wait()
    to_gains.wait()
    to_duals.wait()


def near_kernel(count, ref, duals_ref, gains_out, duals_out, poly_out, gains, duals, poly, sems):
    outs = (gains_out, duals_out, poly_out)
    put_half(count, False, ref, 64, 32, duals_ref, outs, (gains, duals, poly), sems)


def far_kernel(count, ref, duals_ref, _g, _d, _p, gains_out, duals_out, poly_out, gains, duals, poly, sems):
    outs = (gains_out, duals_out, poly_out)
    put_half(count, True, ref, 48, 16, duals_ref, outs, (gains, duals, poly), sems)


def exchanged(x, axis):
    return lax.all_to_all(x, axis, split_axis=0, concat_axis=0, tiled=True)


TIMES = ("c", "r1", "g", "r0")


def shards(visibilities, coherencies, pairs, gains_start, duals_start, poly_start):
    freqs = lax.axis_size("freq")
    times = lax.axis_size(TIMES)
    count = CHANS * freqs
    sums_shape = (CUTS, 12 * 8, LANES)
    tiles = (64, LANES)
    share = (16, LANES)
    work = pltpu.VMEM((2 * SOURCES * 24, ROWS), F32)
    quarters = (CUTS, 24, LANES)

    sent, own = call(
        pack_kernel,
        [(SOURCES, 32, ROWS), tiles],
        gains_start,
        coherencies,
        visibilities,
        pairs,
        fast=[],
        limit=60 << 20,
        scratch=[pltpu.VMEM((CHANS, 64, ROWS), F32)],
        name="pack",
    )
    rows = exchanged(sent, ("c", "g")).reshape(SOURCES * 32, ROWS)
    block = (CHANS, 8, DIRS, STATIONS)
    full = (POLY, 8, DIRS, STATIONS)
    sums, hot, model, duals_start, poly_start = call(
        start_kernel,
        [sums_shape, (STATIONS, 2 * SOURCES * ROWS), tiles, block, full],
        rows,
        own,
        duals_start,
        poly_start,
        fast=[0, 1],
        far=[2, 3],
        kinds=[F32, BF16, F32, F32, F32],
        scratch=[
            pltpu.VMEM((2 * SOURCES * 16, ROWS), F32),
            work,
            pltpu.VMEM(quarters, F32),
            pltpu.SemaphoreType.DMA((2,)),
        ],
        name="start",
    )
    sums = exchanged(sums, ("r1", "r0"))
    change, cut, at = call(
        functools.partial(middle_kernel, 12.0, count),
        [(GROUPS, *tiles), (3, *share), (2 * SOURCES * 16, ROWS)],
        sums,
        own,
        duals_start,
        poly_start,
        rows,
        hot,
        model,
        scratch=[pltpu.VMEM(tiles, F32), pltpu.VMEM((2, *tiles), F32)],
        name="middle",
    )
    change = exchanged(change, "g")
    sums = call(second_kernel, quarters, change, rows, hot, at, scratch=[work], name="second")
    sums = exchanged(sums, ("r1", "r0"))
    mixed = call(
        functools.partial(last_kernel, 6.0),
        (freqs * CHANS, 8, LANES),
        sums,
        cut,
        scratch=[pltpu.VMEM((24, LANES), F32), pltpu.VMEM((2, 8, LANES), F32)],
        name="last",
    )
    mixed = exchanged(mixed, ("freq", "c"))
    members = times // CHANS
    copies = call(functools.partial(joined_kernel, fit_weights(count)), (members, 64, LANES), mixed, name="joined")
    everything = exchanged(copies, ("r1", "g", "r0"))
    other = lax.ppermute(everything[:, 16:], "freq", [(i, i ^ 1) for i in range(freqs)])
    outs = (pltpu.HBM(block, F32), pltpu.HBM(block, F32), pltpu.HBM(full, F32))
    held = [pltpu.VMEM((n, HALF, DIRS, STATIONS), F32) for n in (CHANS, CHANS, POLY)]
    options = dict(
        out_shape=outs,
        out_specs=(HBM, HBM, HBM),
        scratch_shapes=[*held, pltpu.SemaphoreType.DMA((3,))],
        compiler_params=pltpu.CompilerParams(vmem_limit_bytes=12 << 20),
    )
    duals_start = in_vmem(duals_start)
    halves = pl.pallas_call(
        functools.partial(near_kernel, count),
        in_specs=[VMEM, VMEM],
        cost_estimate=pl.CostEstimate(flops=1000000, bytes_accessed=2000000, transcendentals=0),
        name="near",
        **options,
    )(in_vmem(everything.reshape(members * 64, LANES)), duals_start)
    return pl.pallas_call(
        functools.partial(far_kernel, count),
        in_specs=[VMEM, VMEM, HBM, HBM, HBM],
        input_output_aliases={2: 0, 3: 1, 4: 2},
        name="far",
        **options,
    )(in_vmem(other.reshape(members * 48, LANES)), duals_start, *halves)


def solution(mesh):
    freqs = mesh.shape["freq"]
    fine = Mesh(mesh.devices.reshape(freqs, CHANS, 2, GROUPS, 2), ("freq", *TIMES))
    placed = (
        P("freq", None, TIMES),
        P("freq", None, None, TIMES),
        P(None, TIMES),
        P("freq", None, None, None),
        P("freq", None, None, None),
        P(),
    )
    return jax.shard_map(
        shards,
        mesh=fine,
        in_specs=placed,
        out_specs=(P("freq", None, None, None), P("freq", None, None, None), P()),
        check_vma=False,
    )
```

```python
import functools

import jax
import jax.numpy as jnp
import numpy as np
from jax import lax
from jax.experimental import pallas as pl
from jax.experimental.pallas import tpu as pltpu
from jax.sharding import Mesh
from jax.sharding import PartitionSpec as P

ITERS = 2
RHO = 16.0
CHANS = 2
DIRS = 8
STATIONS = 512
ROWS = 128
POLY = 4
LANES = 128
CUTS = STATIONS // LANES
GROUPS = 4
PAIR = DIRS // GROUPS
SOURCES = CHANS * GROUPS
HALF = 4
F32 = jnp.float32
BF16 = jnp.bfloat16


def adjoint(matrix):
    re, im = matrix
    return ([re[0], re[2], re[1], re[3]], [-im[0], -im[2], -im[1], -im[3]])


def product(left, right):
    lr, li = left
    rr, ri = right
    out_re, out_im = [], []
    for row in range(2):
        for col in range(2):
            a = 2 * row
            out_re.append(lr[a] * rr[col] - li[a] * ri[col] + lr[a + 1] * rr[col + 2] - li[a + 1] * ri[col + 2])
            out_im.append(lr[a] * ri[col] + li[a] * rr[col] + lr[a + 1] * ri[col + 2] + li[a + 1] * rr[col + 2])
    return (out_re, out_im)


def normal(matrix):
    re, im = matrix
    return [
        re[0] ** 2 + im[0] ** 2 + re[1] ** 2 + im[1] ** 2,
        re[2] ** 2 + im[2] ** 2 + re[3] ** 2 + im[3] ** 2,
        re[0] * re[2] + im[0] * im[2] + re[1] * re[3] + im[1] * im[3],
        im[0] * re[2] - re[0] * im[2] + im[1] * re[3] - re[1] * im[3],
    ]


def two_parts(x):
    high = x.astype(BF16)
    low = (x - high.astype(F32)).astype(BF16)
    return jnp.concatenate([high, low], axis=0)


VMEM = pl.BlockSpec(memory_space=pltpu.VMEM)
HBM = pl.BlockSpec(memory_space=pltpu.HBM)


def in_hbm(x):
    return pltpu.with_memory_space_constraint(x, pltpu.MemorySpace.HBM)


def in_vmem(x):
    return pltpu.with_memory_space_constraint(x, pltpu.MemorySpace.VMEM)


def call(kernel, outs, *args, scratch=(), fast=None, kinds=None, far=(), limit=12 << 20, name=None):
    fast = range(len(args)) if fast is None else fast
    args = [in_vmem(a) if n in fast else in_hbm(a) if n in far else a for n, a in enumerate(args)]
    many = isinstance(outs, list)
    kinds = kinds or [F32] * len(outs)
    return pl.pallas_call(
        kernel,
        out_shape=tuple(pltpu.VMEM(o, t) for o, t in zip(outs, kinds)) if many else pltpu.VMEM(outs, F32),
        in_specs=[HBM if n in far else VMEM for n in range(len(args))],
        out_specs=tuple(VMEM for _ in outs) if many else VMEM,
        scratch_shapes=list(scratch),
        compiler_params=pltpu.CompilerParams(vmem_limit_bytes=limit),
        name=name,
    )(*args)


def basis_of(channel, count):
    x = (2.0 * channel.astype(F32) + 1.0) / count - 1.0
    return [1.0 + 0.0 * x, x, 1.5 * x * x - 0.5, 2.5 * x * x * x - 1.5 * x]


def fit_weights(count):
    x = (2.0 * np.arange(count) + 1.0) / count - 1.0
    basis = np.stack([np.ones_like(x), x, 1.5 * x * x - 0.5, 2.5 * x**3 - 1.5 * x], axis=1)
    return np.linalg.solve(basis.T @ basis, basis.T)


def split(parts):
    return (parts[:4], parts[4:])


def flat(matrix):
    return matrix[0] + matrix[1]


def pack_kernel(gains_ref, coh_ref, vis_ref, pairs_ref, out_ref, own_ref, sky):
    station = lax.broadcasted_iota(jnp.int32, (STATIONS, ROWS), 0)
    hot = [jnp.where(station == pairs_ref[i : i + 1, :], 1.0, 0.0) for i in range(2)]
    hot = jnp.concatenate(hot, axis=1).astype(BF16)
    rows = gains_ref[...].reshape(CHANS * 8 * DIRS, STATIONS)
    found = jnp.dot(two_parts(rows), hot, preferred_element_type=F32)
    found = found[: rows.shape[0]] + found[rows.shape[0] :]
    names = jnp.concatenate(
        [pairs_ref[0:2, :].astype(F32), jnp.zeros((6, ROWS), F32)],
        axis=0,
    )
    for c in range(CHANS):
        at = [found[(c * 8 + i) * DIRS : (c * 8 + i + 1) * DIRS] for i in range(8)]
        first = split([a[:, :ROWS] for a in at])
        second = split([a[:, ROWS:] for a in at])
        parts = [coh_ref[c, i].astype(F32) for i in range(8)]
        for i in range(8):
            sky[c, pl.ds(i * DIRS, DIRS), :] = parts[i]
        model = flat(product(product(first, split(parts)), adjoint(second)))
        rest = vis_ref[c] - jnp.concatenate([jnp.sum(m, axis=0, keepdims=True) for m in model], axis=0)
        for g in range(GROUPS):
            for d in range(PAIR):
                out_ref[c * GROUPS + g, pl.ds(d * 8, 8), :] = sky[c, pl.ds(d * GROUPS + g, 8, stride=DIRS), :]
            out_ref[c * GROUPS + g, pl.ds(16, 8), :] = rest
            out_ref[c * GROUPS + g, pl.ds(24, 8), :] = names
    _, c, g, _ = place_of()
    for i in range(8):
        to_rows(gains_ref[c, i], i, g, own_ref)


def place_of():
    own = lax.axis_index("r1") * 2 + lax.axis_index("r0")
    return lax.axis_index("freq"), lax.axis_index("c"), lax.axis_index("g"), own


def to_rows(tile, i, g, put):
    sublane = lax.broadcasted_iota(jnp.int32, (DIRS, STATIONS), 0)
    for d in range(PAIR):
        row = jnp.sum(jnp.where(sublane == d * GROUPS + g, tile, 0.0), axis=0, keepdims=True)
        for q in range(CUTS):
            put[pl.ds(i * 8 + q * PAIR + d, 1), :] = row[:, q * LANES : (q + 1) * LANES]


def by_component(gains_ref):
    rows = jnp.concatenate(
        [
            jnp.concatenate(
                [gains_ref[pl.ds(q * PAIR + d, 8, stride=8), :] for q in range(CUTS)], axis=1
            )
            for d in range(PAIR)
        ],
        axis=0,
    )
    return two_parts(rows)


def look_up(parts, hot, at_ref, block):
    found = jnp.dot(parts, hot, preferred_element_type=F32)
    found = found[:16] + found[16:]
    for b in range(hot.shape[1] // ROWS):
        at_ref[pl.ds((block + b) * 16, 16), :] = found[:, b * ROWS : (b + 1) * ROWS]


def ends(at_ref, d):
    first = [at_ref[pl.ds(d * 8 + i, SOURCES, stride=16), :] for i in range(8)]
    second = [at_ref[pl.ds(SOURCES * 16 + d * 8 + i, SOURCES, stride=16), :] for i in range(8)]
    return split(first), split(second)


def sky_of(rows_ref, d):
    return split([rows_ref[pl.ds(d * 8 + i, SOURCES, stride=32), :] for i in range(8)])


def summed(rest, rows_ref, at_ref, hot_ref, terms, total_ref):
    half = SOURCES * 24
    for d in range(PAIR):
        first, second = ends(at_ref, d)
        sky = sky_of(rows_ref, d)
        left = product(first, sky)
        right = product(sky, adjoint(second))
        ahead = flat(product(rest, adjoint(right))) + normal(right)
        behind = flat(product(adjoint(rest), left)) + normal(adjoint(left))
        for i in range(12):
            terms[pl.ds(d * 12 + i, SOURCES, stride=24), :] = ahead[i]
            terms[pl.ds(half + d * 12 + i, SOURCES, stride=24), :] = behind[i]
    wide = jnp.concatenate([terms[pl.ds(b * 24, 24), :] for b in range(2 * SOURCES)], axis=1)
    total = lax.dot_general(
        two_parts(wide), hot_ref[...], (((1,), (1,)), ((), ())), preferred_element_type=F32
    )
    total = total[:24] + total[24:]
    for q in range(CUTS):
        total_ref[q] = total[:, q * LANES : (q + 1) * LANES]


def model_of(rows_ref, at_ref):
    model = None
    for d in range(PAIR):
        first, second = ends(at_ref, d)
        part = flat(product(product(first, sky_of(rows_ref, d)), adjoint(second)))
        model = part if model is None else [a + b for a, b in zip(model, part)]
    return model


def start_kernel(
    rows_ref,
    own_ref,
    duals_far,
    poly_far,
    out_ref,
    hot_ref,
    model_ref,
    duals_ref,
    poly_ref,
    at,
    terms,
    total,
    sems,
):
    loads = [
        pltpu.make_async_copy(duals_far, duals_ref, sems.at[0]),
        pltpu.make_async_copy(poly_far, poly_ref, sems.at[1]),
    ]
    for load in loads:
        load.start()
    shape = (STATIONS // 16, 16, ROWS)
    station = lax.broadcasted_iota(jnp.int32, (STATIONS, ROWS), 0).astype(jnp.int16).reshape(shape)

    def marked(name):
        wide = jnp.broadcast_to(name.astype(jnp.int32), (16, ROWS)).astype(jnp.int16)
        mark = jnp.where(station == wide[None], jnp.ones((), BF16), jnp.zeros((), BF16))
        return mark.reshape(STATIONS, ROWS)

    parts = by_component(own_ref)
    for b in range(0, 2 * SOURCES, 2):
        hot = []
        for n in (b, b + 1):
            end, source = n // SOURCES, n % SOURCES
            hot.append(marked(rows_ref[pl.ds(source * 32 + 24 + end, 1), :]))
        hot = jnp.concatenate(hot, axis=1)
        hot_ref[:, b * ROWS : (b + 2) * ROWS] = hot
        look_up(parts, hot, at, b)
    rest = split([rows_ref[pl.ds(16 + i, SOURCES, stride=32), :] for i in range(8)])
    summed(rest, rows_ref, at, hot_ref, terms, total)
    for q in range(CUTS):
        for d in range(PAIR):
            part = total[q, pl.ds(d * 12, 12), :]
            for n in range(out_ref.shape[0]):
                out_ref[n, pl.ds(q * PAIR + d, 12, stride=8), :] = part
    model = model_of(rows_ref, at)
    for i in range(8):
        model_ref[pl.ds(i * 8, 8), :] = model[i]
    for load in loads:
        load.wait()


def stepped(total, gains, duals, prior, damping):
    way = [total[i] - duals[i] - RHO * (gains[i] - prior[i]) for i in range(8)]
    top, bottom, cross_re, cross_im = total[8:]
    shift = damping * 0.5 * (top + bottom) + RHO
    upper = top + shift
    lower = bottom + shift
    scale = 1.0 / (upper * lower - cross_re * cross_re - cross_im * cross_im)
    zeros = jnp.zeros_like(scale)
    inverse = (
        [lower * scale, -cross_re * scale, -cross_re * scale, upper * scale],
        [zeros, -cross_im * scale, cross_im * scale, zeros],
    )
    step = flat(product(split(way), inverse))
    return [gains[i] + step[i] for i in range(8)]


def middle_kernel(
    damping,
    count,
    arrived,
    own_ref,
    duals_ref,
    poly_ref,
    rows_ref,
    hot_ref,
    model_ref,
    out_ref,
    cut_ref,
    at_ref,
    gains_ref,
    other_ref,
):
    freq, c, g, own = place_of()
    basis = basis_of(freq * CHANS + c, count)
    for i in range(8):
        to_rows(duals_ref[c, i], i, g, other_ref.at[0])
        to_rows(sum(basis[j] * poly_ref[j, i] for j in range(POLY)), i, g, other_ref.at[1])
    total = []
    for i in range(12):
        value = arrived[0, pl.ds(i * 8, 8), :]
        for n in range(1, arrived.shape[0]):
            value = value + arrived[n, pl.ds(i * 8, 8), :]
        total.append(value)
    start = [[ref[pl.ds(i * 8, 8), :] for i in range(8)] for ref in (own_ref, other_ref.at[0], other_ref.at[1])]
    new = stepped(total, *start, damping)
    for i in range(8):
        gains_ref[pl.ds(i * 8, 8), :] = new[i]
        for n, tile in enumerate((new[i], start[1][i], start[2][i])):
            chosen = tile[:PAIR]
            for q in range(1, CUTS):
                chosen = jnp.where(own == q, tile[q * PAIR : (q + 1) * PAIR], chosen)
            cut_ref[n, pl.ds(i, PAIR, stride=8), :] = chosen
    look_up(by_component(gains_ref), hot_ref[...], at_ref, 0)
    model = model_of(rows_ref, at_ref)
    for i in range(8):
        change = model_ref[pl.ds(i * 8, 8), :] - model[i]
        for n in range(out_ref.shape[0]):
            out_ref[n, pl.ds(i * 8, 8), :] = change


def second_kernel(arrived, rows_ref, hot_ref, at_ref, out_ref, terms):
    rest = []
    for i in range(8):
        value = rows_ref[pl.ds(16 + i, SOURCES, stride=32), :]
        for n in range(arrived.shape[0]):
            value = value + arrived[n, pl.ds(i * 8, 8), :]
        rest.append(value)
    summed(split(rest), rows_ref, at_ref, hot_ref, terms, out_ref)


def last_kernel(damping, arrived, own_ref, out_ref, total_ref, mixed_ref):
    value = arrived[0]
    for n in range(1, arrived.shape[0]):
        value = value + arrived[n]
    total_ref[...] = value
    total = [total_ref[pl.ds(i, PAIR, stride=12), :] for i in range(12)]
    gains, duals, prior = [[own_ref[n, pl.ds(i, PAIR, stride=8), :] for i in range(8)] for n in range(3)]
    new = stepped(total, gains, duals, prior, damping)
    for i in range(8):
        mixed_ref[i // HALF, pl.ds(i % HALF, PAIR, stride=HALF), :] = new[i] + duals[i] / RHO
    for n in range(out_ref.shape[0]):
        out_ref[n] = mixed_ref[n // CHANS % 2]


def joined_kernel(weights, arrived, out_ref):
    freq = lax.axis_index("freq")
    twin = freq + 1 - 2 * (freq % 2)
    parts = [arrived[f * CHANS + c] for f in (freq, twin) for c in range(CHANS)]
    mixed = [arrived[n] for n in range(arrived.shape[0])]
    for j in range(POLY):
        total = float(weights[j, 0]) * mixed[0]
        for n in range(1, len(mixed)):
            total = total + float(weights[j, n]) * mixed[n]
        parts.append(total)
    for n in range(out_ref.shape[0]):
        for k, part in enumerate(parts):
            out_ref[n, pl.ds(k * 8, 8), :] = part


def tile_of(ref, q, row, size):
    place = (q // 2) * 8 + q % 2
    return jnp.concatenate(
        [ref[pl.ds(place * size + row + d * HALF, GROUPS, stride=2 * size), :] for d in range(PAIR)], axis=0
    )


def put_half(count, far, ref, size, poly_at, duals_ref, outs, held, sems):
    freq = lax.axis_index("freq")
    side = 1 - freq % 2 if far else freq % 2
    basis = [basis_of(freq * CHANS + c, count) for c in range(CHANS)]
    gains, duals, poly = held
    comps = pl.ds(HALF * side, HALF)
    to_poly = pltpu.make_async_copy(poly, outs[2].at[:, comps], sems.at[0])
    to_rest = [
        [pltpu.make_async_copy(held[n].at[c], outs[n].at[c, comps], sems.at[1 + 2 * c + n]) for n in range(2)]
        for c in range(CHANS)
    ]
    for i in range(HALF):
        for j in range(POLY):
            for q in range(CUTS):
                poly[j, i, :, q * LANES : (q + 1) * LANES] = tile_of(ref, q, poly_at + j * 8 + i, size)
    to_poly.start()
    for c in range(CHANS):
        for i in range(HALF):
            mixed = jnp.concatenate([tile_of(ref, q, c * 8 + i, size) for q in range(CUTS)], axis=1)
            gains[c, i] = mixed - duals_ref[c, HALF * side + i] / RHO
            duals[c, i] = RHO * (mixed - sum(basis[c][j] * poly[j, i] for j in range(POLY)))
        for copy in to_rest[c]:
            copy.start()
    to_poly.wait()
    for copies in to_rest:
        for copy in copies:
            copy.wait()


def near_kernel(count, ref, duals_ref, gains_out, duals_out, poly_out, gains, duals, poly, sems):
    outs = (gains_out, duals_out, poly_out)
    put_half(count, False, ref, 64, 32, duals_ref, outs, (gains, duals, poly), sems)


def far_kernel(count, ref, duals_ref, _g, _d, _p, gains_out, duals_out, poly_out, gains, duals, poly, sems):
    outs = (gains_out, duals_out, poly_out)
    put_half(count, True, ref, 48, 16, duals_ref, outs, (gains, duals, poly), sems)


def exchanged(x, axis):
    return lax.all_to_all(x, axis, split_axis=0, concat_axis=0, tiled=True)


TIMES = ("c", "r1", "g", "r0")


def shards(visibilities, coherencies, pairs, gains_start, duals_start, poly_start):
    freqs = lax.axis_size("freq")
    times = lax.axis_size(TIMES)
    count = CHANS * freqs
    sums_shape = (CUTS, 12 * 8, LANES)
    tiles = (64, LANES)
    share = (16, LANES)
    work = pltpu.VMEM((2 * SOURCES * 24, ROWS), F32)
    quarters = (CUTS, 24, LANES)

    sent, own = call(
        pack_kernel,
        [(SOURCES, 32, ROWS), tiles],
        gains_start,
        coherencies,
        visibilities,
        pairs,
        fast=[],
        limit=60 << 20,
        scratch=[pltpu.VMEM((CHANS, 64, ROWS), F32)],
        name="pack",
    )
    rows = exchanged(sent, ("c", "g")).reshape(SOURCES * 32, ROWS)
    block = (CHANS, 8, DIRS, STATIONS)
    full = (POLY, 8, DIRS, STATIONS)
    sums, hot, model, duals_start, poly_start = call(
        start_kernel,
        [sums_shape, (STATIONS, 2 * SOURCES * ROWS), tiles, block, full],
        rows,
        own,
        duals_start,
        poly_start,
        fast=[0, 1],
        far=[2, 3],
        kinds=[F32, BF16, F32, F32, F32],
        scratch=[
            pltpu.VMEM((2 * SOURCES * 16, ROWS), F32),
            work,
            pltpu.VMEM(quarters, F32),
            pltpu.SemaphoreType.DMA((2,)),
        ],
        name="start",
    )
    sums = exchanged(sums, ("r1", "r0"))
    change, cut, at = call(
        functools.partial(middle_kernel, 12.0, count),
        [(GROUPS, *tiles), (3, *share), (2 * SOURCES * 16, ROWS)],
        sums,
        own,
        duals_start,
        poly_start,
        rows,
        hot,
        model,
        scratch=[pltpu.VMEM(tiles, F32), pltpu.VMEM((2, *tiles), F32)],
        name="middle",
    )
    change = exchanged(change, "g")
    sums = call(second_kernel, quarters, change, rows, hot, at, scratch=[work], name="second")
    sums = exchanged(sums, ("r1", "r0"))
    mixed = call(
        functools.partial(last_kernel, 6.0),
        (freqs * CHANS, 8, LANES),
        sums,
        cut,
        scratch=[pltpu.VMEM((24, LANES), F32), pltpu.VMEM((2, 8, LANES), F32)],
        name="last",
    )
    mixed = exchanged(mixed, ("freq", "c"))
    members = times // CHANS
    copies = call(functools.partial(joined_kernel, fit_weights(count)), (members, 64, LANES), mixed, name="joined")
    everything = exchanged(copies, ("r1", "g", "r0"))
    other = lax.ppermute(everything[:, 16:], "freq", [(i, i ^ 1) for i in range(freqs)])
    outs = (pltpu.HBM(block, F32), pltpu.HBM(block, F32), pltpu.HBM(full, F32))
    held = [pltpu.VMEM((n, HALF, DIRS, STATIONS), F32) for n in (CHANS, CHANS, POLY)]
    options = dict(
        out_shape=outs,
        out_specs=(HBM, HBM, HBM),
        scratch_shapes=[*held, pltpu.SemaphoreType.DMA((5,))],
        compiler_params=pltpu.CompilerParams(vmem_limit_bytes=12 << 20),
    )
    duals_start = in_vmem(duals_start)
    halves = pl.pallas_call(
        functools.partial(near_kernel, count),
        in_specs=[VMEM, VMEM],
        cost_estimate=pl.CostEstimate(flops=1000000, bytes_accessed=2000000, transcendentals=0),
        name="near",
        **options,
    )(in_vmem(everything.reshape(members * 64, LANES)), duals_start)
    return pl.pallas_call(
        functools.partial(far_kernel, count),
        in_specs=[VMEM, VMEM, HBM, HBM, HBM],
        input_output_aliases={2: 0, 3: 1, 4: 2},
        name="far",
        **options,
    )(in_vmem(other.reshape(members * 48, LANES)), duals_start, *halves)


def solution(mesh):
    freqs = mesh.shape["freq"]
    fine = Mesh(mesh.devices.reshape(freqs, CHANS, 2, GROUPS, 2), ("freq", *TIMES))
    placed = (
        P("freq", None, TIMES),
        P("freq", None, None, TIMES),
        P(None, TIMES),
        P("freq", None, None, None),
        P("freq", None, None, None),
        P(),
    )
    return jax.shard_map(
        shards,
        mesh=fine,
        in_specs=placed,
        out_specs=(P("freq", None, None, None), P("freq", None, None, None), P()),
        check_vma=False,
    )
```
